256 devices in a mesh: rows: 32 (over z, y), cols: 8 (over x, core).
Axes of the slice: x: 4, y: 4, z: 8, core: 2. Of those that a mesh axis runs over, the one named last changes fastest.
Arguments:
- matrix: float32 [32768, 10, 1024], P('rows', None, 'cols'), may hold values from -6 to 6
Outputs:
- reduced: float32 [32768, 10, 1024], P('rows', None, 'cols')
- top_rows: float32 [256, 10, 1024], P(None, None, 'cols')
The draws below stay inside these ranges and needn't reach their ends.
All inputs are finite; a program needn't handle non-finite values.
Results may differ from the reference program's by a relative error of at most 0.0001.
Values sent between devices are 32-bit elements; how exact they have to be, the bound alone decides.
No kernel may reach another device: no remote copies, remote signals or barrier semaphores. Data moves between devices by JAX's collectives and lax.ppermute only.
A program may use at most 64 MiB of HBM per device.

```python
import jax
import jax.numpy as jnp
from jax import lax

BLK = 128
ROWS_DEV = 1024
ROUNDS = 10
ROWS = 32768
WIDE = 1024
N_ROWS = 32


def block_scale(key, extent, pieces, least, largest):
    loudness, own = 1.0, jax.random.fold_in(key, 6)
    for axis_at, parts in pieces:
        draws = jnp.exp(jax.random.uniform(jax.random.fold_in(own, axis_at), (parts,), jnp.float32, least / len(pieces), largest / len(pieces)))
        loudness = loudness * jnp.repeat(draws, extent[axis_at] // parts).reshape([-1 if axis == axis_at else 1 for axis in range(len(extent))])
    return loudness


def noise(stream_key, dims, width, reach, cuts=(), dtype=jnp.bfloat16):
    values = jax.random.normal(stream_key, dims, jnp.float32) * width
    if len(cuts) > 0:
        values = block_scale(stream_key, dims, cuts, -0.22, 0.18) * values
    return jnp.clip(values, min=-reach, max=reach).astype(dtype)


def setup_inputs(seed: int = 0) -> dict:
    streams_of = jax.random.split(jax.random.key(seed), 2)
    matrix = noise(streams_of[0], (ROWS, ROUNDS, WIDE), 1.0, 6.0, ((0, 32), (2, 8)), jnp.float32)
    return {"matrix": matrix}


PRECISE = lax.Precision.HIGHEST

def reference(matrix):
    columns = matrix.reshape(ROWS, ROUNDS * WIDE)
    panels = columns[:, :2 * BLK]
    stacked = columns.reshape(N_ROWS, ROWS_DEV, ROUNDS * WIDE)

    def accumulate(total, slab):
        term = jnp.dot(slab[:, :2 * BLK].T.astype(jnp.float32), slab.astype(jnp.float32), precision=PRECISE, preferred_element_type=jnp.float32)
        return (total + term, None)
    cross, unused = lax.scan(accumulate, jnp.zeros((2 * BLK, ROUNDS * WIDE), jnp.float32), stacked)
    gram = cross[:, :2 * BLK]
    triangle = jnp.linalg.cholesky(gram)
    top_rows = jax.scipy.linalg.solve_triangular(triangle, cross, lower=True)
    coefficients = jax.scipy.linalg.solve_triangular(triangle, top_rows, trans=1, lower=True)
    reduced = columns - jnp.dot(panels.astype(jnp.float32), coefficients.astype(jnp.float32), precision=PRECISE, preferred_element_type=jnp.float32)
    return (reduced.reshape(ROWS, ROUNDS, WIDE), top_rows.reshape(2 * BLK, ROUNDS, WIDE))
```

```python
import functools

import jax
import jax.numpy as jnp
from jax import lax
from jax.experimental import pallas as pl
from jax.experimental.pallas import tpu as pltpu
from jax.sharding import Mesh, PartitionSpec as P

PRECISE = lax.Precision.HIGHEST
NZ, NY, NX, NC = 8, 4, 4, 2


def dot(left, right, dims=(((1,), (0,)), ((), ()))):
    return lax.dot_general(left, right, dims, precision=PRECISE, preferred_element_type=jnp.float32)


def relay(own):
    x = lax.axis_index("x")
    half = own.shape[0] // 2
    low, high = own[:half], own[half:]
    up = [(0, 1)]
    down = [(0, 3)]
    s_up = lax.ppermute(low, "x", up)
    s_down = lax.ppermute(high, "x", down)
    t_up = lax.ppermute(jnp.where(x == 0, high, s_up), "x", [(0, 1), (1, 2)])
    t_down = lax.ppermute(jnp.where(x == 0, low, s_down), "x", [(0, 3), (3, 2)])
    got_low = jnp.where(x == 0, low, jnp.where(x == 1, s_up, jnp.where(x == 2, t_up, t_down)))
    got_high = jnp.where(x == 0, high, jnp.where(x == 1, t_up, jnp.where(x == 2, t_down, s_down)))
    mine = jnp.concatenate([got_low, got_high], axis=0)
    other = lax.ppermute(mine, "c", [(0, 1), (1, 0)])
    core = lax.axis_index("c")
    first = jnp.where(core == 0, mine, other)
    second = jnp.where(core == 0, other, mine)
    return jnp.concatenate([first, second], axis=1)


def gram_kernel(p_ref, g_ref):
    p = p_ref[...]
    g_ref[...] = dot(p.T, p)


def gram_of(panels):
    n, w = panels.shape
    return pl.pallas_call(
        gram_kernel,
        out_shape=jax.ShapeDtypeStruct((w, w), jnp.float32),
        name="gram",
    )(panels)


def cross_kernel(p_ref, c_ref, o_ref, pt_ref):
    @pl.when(pl.program_id(0) == 0)
    def _():
        pt_ref[...] = p_ref[...].T

    pair = jnp.concatenate([c_ref[0], c_ref[1]], axis=1)
    o_ref[...] = dot(pt_ref[...], pair)


def cross_of(panels, columns):
    rounds, n, k = columns.shape
    w = panels.shape[1]
    return pl.pallas_call(
        cross_kernel,
        grid=(rounds // 2,),
        in_specs=[
            pl.BlockSpec((n, w), lambda i: (0, 0)),
            pl.BlockSpec((2, n, k), lambda i: (i, 0, 0)),
        ],
        out_specs=pl.BlockSpec((w, 2 * k), lambda i: (0, i)),
        out_shape=jax.ShapeDtypeStruct((w, rounds * k), jnp.float32),
        scratch_shapes=[pltpu.VMEM((w, n), jnp.float32)],
        name="cross",
    )(panels, columns)


def update_kernel(w_ref, x_ref, p_ref, c_ref, red_ref, top_ref):
    inverse = w_ref[...]
    top = dot(inverse, x_ref[...])
    k = c_ref.shape[2]
    top_ref[0] = top[:, :k]
    top_ref[1] = top[:, k:]
    coefficients = dot(inverse.T, top)
    fit = dot(p_ref[...], coefficients)
    red_ref[0] = c_ref[0] - fit[:, :k]
    red_ref[1] = c_ref[1] - fit[:, k:]


def update(inverse, cross, panels, columns):
    rounds, n, k = columns.shape
    w = panels.shape[1]
    return pl.pallas_call(
        update_kernel,
        grid=(rounds // 2,),
        in_specs=[
            pl.BlockSpec((w, w), lambda i: (0, 0)),
            pl.BlockSpec((w, 2 * k), lambda i: (0, i)),
            pl.BlockSpec((n, w), lambda i: (0, 0)),
            pl.BlockSpec((2, n, k), lambda i: (i, 0, 0)),
        ],
        out_specs=[
            pl.BlockSpec((2, n, k), lambda i: (i, 0, 0)),
            pl.BlockSpec((2, w, k), lambda i: (i, 0, 0)),
        ],
        out_shape=[
            jax.ShapeDtypeStruct((rounds, n, k), jnp.float32),
            jax.ShapeDtypeStruct((rounds, w, k), jnp.float32),
        ],
        compiler_params=pltpu.CompilerParams(vmem_limit_bytes=48 << 20),
        name="update",
    )(inverse, cross, panels, columns)


def scatter_sum(values, axis, parts):
    rows, width = values.shape
    pieces = lax.all_to_all(values.reshape(parts, rows // parts, width), axis, 0, 0)
    return jnp.sum(pieces, axis=0)


def gather(values, axis, parts):
    rows, width = values.shape
    copies = jnp.broadcast_to(values[None], (parts, rows, width))
    return lax.all_to_all(copies, axis, 0, 0).reshape(parts * rows, width)


def reduce_rows(values):
    part = scatter_sum(values, "y", NY)
    part = scatter_sum(part, "z", NZ)
    part = gather(part, "z", NZ)
    return gather(part, "y", NY)


def shards(matrix):
    columns = jnp.transpose(matrix, (1, 0, 2))
    panels = relay(columns[0])
    gram = reduce_rows(gram_of(panels))
    cross = reduce_rows(cross_of(panels, columns))
    triangle = jnp.linalg.cholesky(gram)
    eye = jnp.eye(gram.shape[0], dtype=jnp.float32)
    inverse = jax.scipy.linalg.solve_triangular(triangle, eye, lower=True)
    reduced, top = update(inverse, cross, panels, columns)
    return jnp.transpose(reduced, (1, 0, 2)), jnp.transpose(top, (1, 0, 2))


def solution(mesh):
    fine = Mesh(mesh.devices.reshape(NZ, NY, NX, NC), ("z", "y", "x", "c"))
    return jax.shard_map(
        shards,
        mesh=fine,
        in_specs=(P(("z", "y"), None, ("x", "c")),),
        out_specs=(P(("z", "y"), None, ("x", "c")), P(None, None, ("x", "c"))),
        check_vma=False,
    )
```

```python
import jax
import jax.numpy as jnp
from jax import lax
from jax.experimental import pallas as pl
from jax.experimental.pallas import tpu as pltpu
from jax.sharding import Mesh, PartitionSpec as P

PRECISE = lax.Precision.HIGHEST
NZ, NY, NX, NC = 8, 4, 4, 2
LANES, SUB = 128, 8
NT = (((1,), (1,)), ((), ()))
VMEM_BYTES = 48 << 20


def dot(left, right, dims=(((1,), (0,)), ((), ()))):
    return lax.dot_general(left, right, dims, precision=PRECISE, preferred_element_type=jnp.float32)


def pick(index, choices):
    value = choices[-1]
    for at in range(len(choices) - 2, -1, -1):
        value = jnp.where(index == at, choices[at], value)
    return value


def relay(own):
    x = lax.axis_index("x")
    half = own.shape[0] // 2
    low, high = own[:half], own[half:]
    up_low = lax.ppermute(low, "x", [(0, 1)])
    down_high = lax.ppermute(high, "x", [(0, 3)])
    up_high = lax.ppermute(high, "x", [(0, 1)])
    down_low = lax.ppermute(low, "x", [(0, 3)])
    on_low = lax.ppermute(up_low, "x", [(1, 2)])
    on_high = lax.ppermute(down_high, "x", [(3, 2)])
    mine_low = pick(x, [low, up_low, on_low, down_low])
    mine_high = pick(x, [high, up_high, on_high, down_high])
    swap = [(0, 1), (1, 0)]
    return mine_low, mine_high, lax.ppermute(mine_low, "c", swap), lax.ppermute(mine_high, "c", swap)


def products_kernel(core_ref, ml_ref, mh_ref, ol_ref, oh_ref, c_ref, o_ref, p_ref, pt_ref):
    i = pl.program_id(0)
    half, k = ml_ref.shape

    @pl.when(i == 0)
    def _():
        first = core_ref[0] == 0
        for rows, m_ref, t_ref in ((slice(0, half), ml_ref, ol_ref), (slice(half, 2 * half), mh_ref, oh_ref)):
            mine, other = m_ref[...], t_ref[...]
            p_ref[rows, :k] = jnp.where(first, mine, other)
            p_ref[rows, k:] = jnp.where(first, other, mine)
        pt_ref[...] = p_ref[...].T
        o_ref[...] = dot(pt_ref[...], p_ref[...])

    @pl.when(i > 0)
    def _():
        o_ref[...] = dot(pt_ref[...], jnp.concatenate([c_ref[0], c_ref[1]], axis=1))


def products(pieces, columns):
    rounds, n, k = columns.shape
    w = 2 * k
    core = lax.axis_index("c").astype(jnp.int32)[None]
    whole = pl.BlockSpec((n // 2, k), lambda i: (0, 0))
    return pl.pallas_call(
        products_kernel,
        grid=(rounds // 2 + 1,),
        in_specs=[pl.BlockSpec(memory_space=pltpu.SMEM)]
        + [whole] * 4
        + [pl.BlockSpec((2, n, k), lambda i: (jnp.maximum(i - 1, 0), 0, 0))],
        out_specs=[pl.BlockSpec((w, w), lambda i: (0, i)), pl.BlockSpec((n, w), lambda i: (0, 0))],
        out_shape=[
            jax.ShapeDtypeStruct((w, w + rounds * k), jnp.float32),
            jax.ShapeDtypeStruct((n, w), jnp.float32),
        ],
        scratch_shapes=[pltpu.VMEM((w, n), jnp.float32)],
        compiler_params=pltpu.CompilerParams(vmem_limit_bytes=VMEM_BYTES),
        name="products",
    )(core, *pieces, columns)


def inverse_root(d):
    y = lax.rsqrt(d)
    return y * (1.5 - 0.5 * d * y * y)


def invert_factor(block, w_ref, row0, col0):
    n = LANES
    tiles = n // SUB
    a = [block[SUB * t:SUB * (t + 1)] for t in range(tiles)]
    lane = lax.broadcasted_iota(jnp.int32, (SUB, LANES), 1)
    sub = lax.broadcasted_iota(jnp.int32, (SUB, LANES), 0)
    b = [jnp.where(lane == sub + SUB * t, 1.0, 0.0).astype(jnp.float32) for t in range(tiles)]

    def across(v, j):
        return jnp.broadcast_to(v[:, j:j + 1], (SUB, LANES))

    def down(v, s):
        return jnp.broadcast_to(v[s:s + 1, :], (SUB, LANES))

    for q in range(n // 4):
        t, s, j = q // 2, (q % 2) * 4, 4 * q
        ra = [down(a[t], s + k) for k in range(4)]
        rb = [down(b[t], s + k) for k in range(4)]
        d = {}
        for x in range(4):
            for y in range(x + 1):
                d[x, y] = across(ra[y], j + x)
                d[y, x] = d[x, y]
        det = 1.0 / (d[0, 0] * d[1, 1] - d[1, 0] * d[1, 0])
        p00, p01, p11 = d[1, 1] * det, -d[1, 0] * det, d[0, 0] * det
        z = [[d[r, 0] * p00 + d[r, 1] * p01, d[r, 0] * p01 + d[r, 1] * p11] for r in (2, 3)]
        s00 = d[2, 2] - (z[0][0] * d[2, 0] + z[0][1] * d[2, 1])
        s01 = d[3, 2] - (z[1][0] * d[2, 0] + z[1][1] * d[2, 1])
        s11 = d[3, 3] - (z[1][0] * d[3, 0] + z[1][1] * d[3, 1])
        sdet = 1.0 / (s00 * s11 - s01 * s01)
        i00, i01, i11 = s11 * sdet, -s01 * sdet, s00 * sdet

        def solve(r):
            u0 = p00 * r[0] + p01 * r[1]
            u1 = p01 * r[0] + p11 * r[1]
            v2 = r[2] - (z[0][0] * r[0] + z[0][1] * r[1])
            v3 = r[3] - (z[1][0] * r[0] + z[1][1] * r[1])
            y2 = i00 * v2 + i01 * v3
            y3 = i01 * v2 + i11 * v3
            return [u0 - (z[0][0] * y2 + z[1][0] * y3), u1 - (z[0][1] * y2 + z[1][1] * y3), y2, y3]

        ya, yb = solve(ra), solve(rb)
        for u in range(t, tiles):
            if u == t and s == 4:
                continue
            c = [across(a[u], j + k) for k in range(4)]
            na, nb = a[u], b[u]
            fa = (c[0] * ya[0] + c[1] * ya[1]) + (c[2] * ya[2] + c[3] * ya[3])
            fb = (c[0] * yb[0] + c[1] * yb[1]) + (c[2] * yb[2] + c[3] * yb[3])
            if u == t:
                a[u] = jnp.where(sub >= 4, na - fa, na)
                b[u] = jnp.where(sub >= 4, nb - fb, nb)
            else:
                a[u], b[u] = na - fa, nb - fb
        k0 = inverse_root(d[0, 0])
        l10 = d[1, 0] * k0
        k1 = inverse_root(d[1, 1] - l10 * l10)
        w0 = k0 * rb[0]
        w1 = k1 * (rb[1] - l10 * w0)
        k2 = inverse_root(s00)
        l32 = s01 * k2
        k3 = inverse_root(s11 - l32 * l32)
        v2 = rb[2] - (z[0][0] * rb[0] + z[0][1] * rb[1])
        v3 = rb[3] - (z[1][0] * rb[0] + z[1][1] * rb[1])
        w2 = k2 * v2
        w3 = k3 * (v3 - l32 * w2)
        for k, w in enumerate((w0, w1, w2, w3)):
            w_ref[row0 + j + k:row0 + j + k + 1, col0:col0 + LANES] = w[0:1]


def factor_kernel(y_ref, g0_ref, g1_ref, g2_ref, g3_ref, p_ref, w_ref, q_ref, g_ref):
    part, h = g0_ref.shape[0], LANES
    y = y_ref[0]
    for step, block in enumerate((g0_ref, g1_ref, g2_ref, g3_ref)):
        at = pl.multiple_of(((y + step) % NY) * part, part)
        g_ref[pl.ds(at, part), :] = block[...]
    invert_factor(g_ref[:h, :h], w_ref, 0, 0)
    w_ref[:h, h:] = jnp.zeros((h, h), jnp.float32)
    w11 = w_ref[:h, :h]
    l21 = dot(g_ref[h:, :h], w11, NT)
    invert_factor(g_ref[h:, h:] - dot(l21, l21, NT), w_ref, h, h)
    w_ref[h:, :h] = -dot(w_ref[h:, h:], dot(l21, w11))
    q_ref[...] = dot(p_ref[...], w_ref[...], NT)


def factor(parts, panels):
    n, w = panels.shape
    y = lax.axis_index("y").astype(jnp.int32)[None]
    vmem = pl.BlockSpec(memory_space=pltpu.VMEM)
    return pl.pallas_call(
        factor_kernel,
        in_specs=[pl.BlockSpec(memory_space=pltpu.SMEM)] + [vmem] * 5,
        out_shape=[jax.ShapeDtypeStruct((w, w), jnp.float32), jax.ShapeDtypeStruct((n, w), jnp.float32)],
        scratch_shapes=[pltpu.VMEM((w, w), jnp.float32)],
        compiler_params=pltpu.CompilerParams(vmem_limit_bytes=VMEM_BYTES),
        name="factor",
    )(y, *parts, panels)


def update_kernel(w_ref, x_ref, q_ref, c_ref, red_ref, top_ref):
    k = c_ref.shape[2]
    top = dot(w_ref[...], x_ref[...])
    fit = dot(q_ref[...], top)
    for at in range(2):
        top_ref[at] = top[:, at * k : (at + 1) * k]
        red_ref[at] = c_ref[at] - fit[:, at * k : (at + 1) * k]


def update(inverse, basis, cross, columns):
    rounds, n, k = columns.shape
    w = inverse.shape[0]
    return pl.pallas_call(
        update_kernel,
        grid=(rounds // 2,),
        in_specs=[
            pl.BlockSpec((w, w), lambda i: (0, 0)),
            pl.BlockSpec((w, 2 * k), lambda i: (0, i)),
            pl.BlockSpec((n, w), lambda i: (0, 0)),
            pl.BlockSpec((2, n, k), lambda i: (i, 0, 0)),
        ],
        out_specs=[
            pl.BlockSpec((2, n, k), lambda i: (i, 0, 0)),
            pl.BlockSpec((2, w, k), lambda i: (i, 0, 0)),
        ],
        out_shape=[
            jax.ShapeDtypeStruct((rounds, n, k), jnp.float32),
            jax.ShapeDtypeStruct((rounds, w, k), jnp.float32),
        ],
        compiler_params=pltpu.CompilerParams(vmem_limit_bytes=VMEM_BYTES),
        name="update",
    )(inverse, cross, basis, columns)


def scatter_sum(values, axis, parts):
    rows, width = values.shape
    pieces = lax.all_to_all(values.reshape(parts, rows // parts, width), axis, 0, 0)
    return jnp.sum(pieces, axis=0)


def gather(values, axis, parts):
    rows, width = values.shape
    copies = jnp.broadcast_to(values[None], (parts, rows, width))
    return lax.all_to_all(copies, axis, 0, 0).reshape(parts * rows, width)


def shards(matrix):
    columns = jnp.transpose(matrix, (1, 0, 2))
    both, panels = products(relay(columns[0]), columns)
    part = scatter_sum(both, "y", NY)
    part = scatter_sum(part, "z", NZ)
    part = gather(part, "z", NZ)
    w = panels.shape[1]
    gram_part, cross_part = part[:, :w], part[:, w:]
    ahead = [lax.ppermute(gram_part, "y", [(y, (y - by) % NY) for y in range(NY)]) for by in (1, 2, 3)]
    inverse, basis = factor([gram_part, *ahead], panels)
    cross = gather(cross_part, "y", NY)
    reduced, top = update(inverse, basis, cross, columns)
    return jnp.transpose(reduced, (1, 0, 2)), jnp.transpose(top, (1, 0, 2))


def solution(mesh):
    fine = Mesh(mesh.devices.reshape(NZ, NY, NX, NC), ("z", "y", "x", "c"))
    return jax.shard_map(
        shards,
        mesh=fine,
        in_specs=(P(("z", "y"), None, ("x", "c")),),
        out_specs=(P(("z", "y"), None, ("x", "c")), P(None, None, ("x", "c"))),
        check_vma=False,
    )
```

```python
import jax
import jax.numpy as jnp
from jax import lax
from jax.experimental import pallas as pl
from jax.experimental.pallas import tpu as pltpu
from jax.sharding import Mesh, PartitionSpec as P

PRECISE = lax.Precision.HIGHEST
NZ, NY, NX, NC = 8, 4, 4, 2
LANES, SUB = 128, 8
NT = (((1,), (1,)), ((), ()))
PARAMS = pltpu.CompilerParams(vmem_limit_bytes=48 << 20)


def dot(left, right, dims=(((1,), (0,)), ((), ()))):
    return lax.dot_general(left, right, dims, precision=PRECISE, preferred_element_type=jnp.float32)


def pick(index, choices):
    value = choices[-1]
    for at in range(len(choices) - 2, -1, -1):
        value = jnp.where(index == at, choices[at], value)
    return value


def spread_x(values):
    return [values] + [lax.ppermute(values, "x", [(0, to)]) for to in (1, 2, 3)]


def swap(values):
    return lax.ppermute(values, "c", [(0, 1), (1, 0)])


def index_of(axis):
    return lax.axis_index(axis).astype(jnp.int32)[None]


SCALAR = pl.BlockSpec(memory_space=pltpu.SMEM)


def whole(shape):
    return pl.BlockSpec(shape, lambda i: (0,) * len(shape))


def place(core_ref, mine_ref, other_ref, p_ref):
    k = mine_ref.shape[1]
    first = core_ref[0] == 0
    mine, other = mine_ref[...], other_ref[...]
    p_ref[:, :k] = jnp.where(first, mine, other)
    p_ref[:, k:] = jnp.where(first, other, mine)


def gram_kernel(core_ref, mine_ref, other_ref, g_ref, p_ref):
    place(core_ref, mine_ref, other_ref, p_ref)
    panels = p_ref[...]
    g_ref[...] = dot(panels.T, panels)


def gram_of(mine, other):
    n, k = mine.shape
    w = 2 * k
    return pl.pallas_call(
        gram_kernel,
        grid=(1,),
        in_specs=[SCALAR, whole((n, k)), whole((n, k))],
        out_specs=whole((w, w)),
        out_shape=jax.ShapeDtypeStruct((w, w), jnp.float32),
        scratch_shapes=[pltpu.VMEM((n, w), jnp.float32)],
        compiler_params=PARAMS,
        name="gram",
    )(index_of("c"), mine, other)


def cross_kernel(core_ref, mine_ref, other_ref, c_ref, o_ref, p_ref, pt_ref):
    @pl.when(pl.program_id(0) == 0)
    def _():
        place(core_ref, mine_ref, other_ref, p_ref)
        pt_ref[...] = p_ref[...].T

    o_ref[...] = dot(pt_ref[...], jnp.concatenate([c_ref[0], c_ref[1]], axis=1))


def cross_of(mine, other, columns):
    rounds, n, k = columns.shape
    w = 2 * k
    return pl.pallas_call(
        cross_kernel,
        grid=(rounds // 2,),
        in_specs=[SCALAR, whole((n, k)), whole((n, k)), pl.BlockSpec((2, n, k), lambda i: (i, 0, 0))],
        out_specs=[pl.BlockSpec((w, w), lambda i: (0, i)), whole((n, w))],
        out_shape=[
            jax.ShapeDtypeStruct((w, rounds * k), jnp.float32),
            jax.ShapeDtypeStruct((n, w), jnp.float32),
        ],
        scratch_shapes=[pltpu.VMEM((w, n), jnp.float32)],
        compiler_params=PARAMS,
        name="cross",
    )(index_of("c"), mine, other, columns)


def inverse_root(d):
    y = lax.rsqrt(d)
    return y * (1.5 - 0.5 * d * y * y)


def invert_factor(block, w_ref, row0, col0):
    n = LANES
    tiles = n // SUB
    a = [block[SUB * t:SUB * (t + 1)] for t in range(tiles)]
    lane = lax.broadcasted_iota(jnp.int32, (SUB, LANES), 1)
    sub = lax.broadcasted_iota(jnp.int32, (SUB, LANES), 0)
    b = [jnp.where(lane == sub + SUB * t, 1.0, 0.0).astype(jnp.float32) for t in range(tiles)]

    def across(v, j):
        return jnp.broadcast_to(v[:, j:j + 1], (SUB, LANES))

    def down(v, s):
        return jnp.broadcast_to(v[s:s + 1, :], (SUB, LANES))

    for q in range(n // 4):
        t, s, j = q // 2, (q % 2) * 4, 4 * q
        ra = [down(a[t], s + k) for k in range(4)]
        rb = [down(b[t], s + k) for k in range(4)]
        d = {}
        for x in range(4):
            for y in range(x + 1):
                d[x, y] = across(ra[y], j + x)
                d[y, x] = d[x, y]
        det = 1.0 / (d[0, 0] * d[1, 1] - d[1, 0] * d[1, 0])
        p00, p01, p11 = d[1, 1] * det, -d[1, 0] * det, d[0, 0] * det
        z = [[d[r, 0] * p00 + d[r, 1] * p01, d[r, 0] * p01 + d[r, 1] * p11] for r in (2, 3)]
        s00 = d[2, 2] - (z[0][0] * d[2, 0] + z[0][1] * d[2, 1])
        s01 = d[3, 2] - (z[1][0] * d[2, 0] + z[1][1] * d[2, 1])
        s11 = d[3, 3] - (z[1][0] * d[3, 0] + z[1][1] * d[3, 1])
        sdet = 1.0 / (s00 * s11 - s01 * s01)
        i00, i01, i11 = s11 * sdet, -s01 * sdet, s00 * sdet

        def solve(r):
            u0 = p00 * r[0] + p01 * r[1]
            u1 = p01 * r[0] + p11 * r[1]
            v2 = r[2] - (z[0][0] * r[0] + z[0][1] * r[1])
            v3 = r[3] - (z[1][0] * r[0] + z[1][1] * r[1])
            y2 = i00 * v2 + i01 * v3
            y3 = i01 * v2 + i11 * v3
            return [u0 - (z[0][0] * y2 + z[1][0] * y3), u1 - (z[0][1] * y2 + z[1][1] * y3), y2, y3]

        ya, yb = solve(ra), solve(rb)
        for u in range(t, tiles):
            if u == t and s == 4:
                continue
            c = [across(a[u], j + k) for k in range(4)]
            na, nb = a[u], b[u]
            fa = (c[0] * ya[0] + c[1] * ya[1]) + (c[2] * ya[2] + c[3] * ya[3])
            fb = (c[0] * yb[0] + c[1] * yb[1]) + (c[2] * yb[2] + c[3] * yb[3])
            if u == t:
                a[u] = jnp.where(sub >= 4, na - fa, na)
                b[u] = jnp.where(sub >= 4, nb - fb, nb)
            else:
                a[u], b[u] = na - fa, nb - fb
        k0 = inverse_root(d[0, 0])
        l10 = d[1, 0] * k0
        k1 = inverse_root(d[1, 1] - l10 * l10)
        w0 = k0 * rb[0]
        w1 = k1 * (rb[1] - l10 * w0)
        k2 = inverse_root(s00)
        l32 = s01 * k2
        k3 = inverse_root(s11 - l32 * l32)
        v2 = rb[2] - (z[0][0] * rb[0] + z[0][1] * rb[1])
        v3 = rb[3] - (z[1][0] * rb[0] + z[1][1] * rb[1])
        w2 = k2 * v2
        w3 = k3 * (v3 - l32 * w2)
        for k, w in enumerate((w0, w1, w2, w3)):
            w_ref[row0 + j + k:row0 + j + k + 1, col0:col0 + LANES] = w[0:1]


def factor_first_kernel(x_ref, *refs):
    grams, (w_ref, l_ref, s_ref, g_ref) = refs[:NX], refs[NX:]
    h = LANES
    for at, gram in enumerate(grams):

        @pl.when(x_ref[0] == at)
        def _(gram=gram):
            g_ref[...] = gram[...]

    invert_factor(g_ref[:h, :h], w_ref, 0, 0)
    l21 = dot(g_ref[h:, :h], w_ref[...], NT)
    l_ref[...] = l21
    s_ref[...] = g_ref[h:, h:] - dot(l21, l21, NT)


def factor_last_kernel(w11_ref, l_ref, s_ref, p_ref, w_ref, q_ref):
    h = LANES
    w11 = w11_ref[...]
    w_ref[:h, :h] = w11
    w_ref[:h, h:] = jnp.zeros((h, h), jnp.float32)
    invert_factor(s_ref[...], w_ref, h, h)
    w_ref[h:, :h] = -dot(w_ref[h:, h:], dot(l_ref[...], w11))
    q_ref[...] = dot(p_ref[...], w_ref[...], NT)


def factor_first(grams):
    w = grams[0].shape[0]
    h = w // 2
    return pl.pallas_call(
        factor_first_kernel,
        grid=(1,),
        in_specs=[SCALAR] + [whole((w, w))] * NX,
        out_specs=[whole((h, h))] * 3,
        out_shape=[jax.ShapeDtypeStruct((h, h), jnp.float32)] * 3,
        scratch_shapes=[pltpu.VMEM((w, w), jnp.float32)],
        compiler_params=PARAMS,
        name="factor_first",
    )(index_of("x"), *grams)


def factor_last(w11, l21, schur, panels):
    n, w = panels.shape
    h = w // 2
    return pl.pallas_call(
        factor_last_kernel,
        grid=(1,),
        in_specs=[whole((h, h))] * 3 + [whole((n, w))],
        out_specs=[whole((w, w)), whole((n, w))],
        out_shape=[jax.ShapeDtypeStruct((w, w), jnp.float32), jax.ShapeDtypeStruct((n, w), jnp.float32)],
        compiler_params=PARAMS,
        name="factor_last",
    )(w11, l21, schur, panels)


def update_kernel(w_ref, x_ref, q_ref, c_ref, red_ref, top_ref):
    k = c_ref.shape[2]
    top = dot(w_ref[...], x_ref[...])
    fit = dot(q_ref[...], top)
    for at in range(2):
        top_ref[at] = top[:, at * k : (at + 1) * k]
        red_ref[at] = c_ref[at] - fit[:, at * k : (at + 1) * k]


def update(inverse, basis, cross, columns):
    rounds, n, k = columns.shape
    w = inverse.shape[0]
    return pl.pallas_call(
        update_kernel,
        grid=(rounds // 2,),
        in_specs=[
            pl.BlockSpec((w, w), lambda i: (0, 0)),
            pl.BlockSpec((w, 2 * k), lambda i: (0, i)),
            pl.BlockSpec((n, w), lambda i: (0, 0)),
            pl.BlockSpec((2, n, k), lambda i: (i, 0, 0)),
        ],
        out_specs=[
            pl.BlockSpec((2, n, k), lambda i: (i, 0, 0)),
            pl.BlockSpec((2, w, k), lambda i: (i, 0, 0)),
        ],
        out_shape=[
            jax.ShapeDtypeStruct((rounds, n, k), jnp.float32),
            jax.ShapeDtypeStruct((rounds, w, k), jnp.float32),
        ],
        compiler_params=PARAMS,
        name="update",
    )(inverse, cross, basis, columns)


def scatter_sum(values, axis, parts):
    rows, width = values.shape
    pieces = lax.all_to_all(values.reshape(parts, rows // parts, width), axis, 0, 0)
    return jnp.sum(pieces, axis=0)


def gather(values, axis, parts):
    rows, width = values.shape
    copies = jnp.broadcast_to(values[None], (parts, rows, width))
    return lax.all_to_all(copies, axis, 0, 0).reshape(parts * rows, width)


def shards(matrix):
    hold = lax.optimization_barrier
    columns = jnp.transpose(matrix, (1, 0, 2))
    own = columns[0]
    arrived = spread_x(own)
    gram = gram_of(own, swap(own))
    rows = ("z", "y")
    gram = scatter_sum(gram, rows, NZ * NY)
    gram, arrived = hold((gram, arrived))
    gram = gather(gram, rows, NZ * NY)
    mine = pick(lax.axis_index("x"), arrived)
    cross, panels = cross_of(mine, swap(mine), columns)
    gram, cross = hold((gram, cross))
    part = scatter_sum(cross, "y", NY)
    first = factor_first(spread_x(gram))
    part, first = hold((part, first))
    part = scatter_sum(part, "z", NZ)
    last = factor_last(*first, panels)
    part, (inverse, basis) = hold((part, last))
    part = gather(part, "z", NZ)
    cross = gather(part, "y", NY)
    reduced, top = update(inverse, basis, cross, columns)
    return jnp.transpose(reduced, (1, 0, 2)), jnp.transpose(top, (1, 0, 2))


def solution(mesh):
    fine = Mesh(mesh.devices.reshape(NZ, NY, NX, NC), ("z", "y", "x", "c"))
    return jax.shard_map(
        shards,
        mesh=fine,
        in_specs=(P(("z", "y"), None, ("x", "c")),),
        out_specs=(P(("z", "y"), None, ("x", "c")), P(None, None, ("x", "c"))),
        check_vma=False,
    )
```

```python
import jax
import jax.numpy as jnp
from jax import lax
from jax.experimental import pallas as pl
from jax.experimental.pallas import tpu as pltpu
from jax.sharding import Mesh, PartitionSpec as P

PRECISE = lax.Precision.HIGHEST
NZ, NY, NX, NC = 8, 4, 4, 2
LANES, SUB = 128, 8
RIDE = 1280
NT = (((1,), (1,)), ((), ()))
PARAMS = pltpu.CompilerParams(vmem_limit_bytes=48 << 20)


def dot(left, right, dims=(((1,), (0,)), ((), ()))):
    return lax.dot_general(left, right, dims, precision=PRECISE, preferred_element_type=jnp.float32)


def pick(index, choices):
    value = choices[-1]
    for at in range(len(choices) - 2, -1, -1):
        value = jnp.where(index == at, choices[at], value)
    return value


def swap(values):
    return lax.ppermute(values, "c", [(0, 1), (1, 0)])


def relay(own):
    x = lax.axis_index("x")
    half = own.shape[0] // 2
    low, high = own[:half], own[half:]
    up_low = lax.ppermute(low, "x", [(0, 1)])
    down_high = lax.ppermute(high, "x", [(0, 3)])
    up_high = lax.ppermute(high, "x", [(0, 1)])
    down_low = lax.ppermute(low, "x", [(0, 3)])
    on_low = lax.ppermute(up_low, "x", [(1, 2)])
    on_high = lax.ppermute(down_high, "x", [(3, 2)])
    mine_low = pick(x, [low, up_low, on_low, down_low])
    mine_high = pick(x, [high, up_high, on_high, down_high])
    return mine_low, mine_high, swap(mine_low), swap(mine_high)


def index_of(axis):
    return lax.axis_index(axis).astype(jnp.int32)[None]


SCALAR = pl.BlockSpec(memory_space=pltpu.SMEM)


def whole(shape):
    return pl.BlockSpec(shape, lambda i: (0,) * len(shape))


def place(core, pieces, p_ref):
    half, k = pieces[0].shape
    first = core == 0
    for at in range(2):
        rows = slice(at * half, (at + 1) * half)
        mine, other = pieces[at][...], pieces[2 + at][...]
        p_ref[rows, :k] = jnp.where(first, mine, other)
        p_ref[rows, k:] = jnp.where(first, other, mine)


def products_kernel(x_ref, core_ref, ml_ref, mh_ref, ol_ref, oh_ref, c_ref, o_ref, p_ref, pt_ref):
    i = pl.program_id(0)
    k = c_ref.shape[2]
    w = 2 * k

    @pl.when(i == 0)
    def _():
        place(core_ref[0], (ml_ref, mh_ref, ol_ref, oh_ref), p_ref)
        pt_ref[...] = p_ref[...].T
        share = NY * SUB
        at = pl.multiple_of((x_ref[0] * NC + core_ref[0]) * share, share)
        gram = dot(pt_ref[pl.ds(at, share), :], p_ref[...])
        o_ref[:, RIDE:] = jnp.zeros((w, LANES), jnp.float32)
        for y in range(NY):
            row = y * (w // NY)
            piece = gram[y * SUB : (y + 1) * SUB]
            o_ref[row : row + SUB, RIDE:] = piece[:, :LANES]
            o_ref[row + SUB : row + 2 * SUB, RIDE:] = piece[:, LANES:]

    lanes = pl.ds(pl.multiple_of(i * w, w), w)
    o_ref[:, lanes] = dot(pt_ref[...], jnp.concatenate([c_ref[0], c_ref[1]], axis=1))


def products(pieces, columns):
    rounds, n, k = columns.shape
    w = 2 * k
    return pl.pallas_call(
        products_kernel,
        grid=(rounds // 2,),
        in_specs=[SCALAR, SCALAR]
        + [whole((n // 2, k))] * 4
        + [pl.BlockSpec((2, n, k), lambda i: (i, 0, 0))],
        out_specs=[whole((w, RIDE + LANES)), whole((n, w))],
        out_shape=[
            jax.ShapeDtypeStruct((w, RIDE + LANES), jnp.float32),
            jax.ShapeDtypeStruct((n, w), jnp.float32),
        ],
        scratch_shapes=[pltpu.VMEM((w, n), jnp.float32)],
        compiler_params=PARAMS,
        name="products",
    )(index_of("x"), index_of("c"), *pieces, columns)


def sum_y_kernel(a_ref, o_ref):
    total = (a_ref[0] + a_ref[1]) + (a_ref[2] + a_ref[3])
    for z in range(NZ):
        o_ref[z, :, :RIDE] = total[z * SUB : (z + 1) * SUB, :RIDE]
        o_ref[z, :, RIDE : RIDE + LANES] = total[:SUB, RIDE:]
        o_ref[z, :, RIDE + LANES :] = total[SUB : 2 * SUB, RIDE:]


def sum_y(pieces):
    out = (NZ, SUB, RIDE + 2 * LANES)
    return pl.pallas_call(
        sum_y_kernel,
        grid=(1,),
        in_specs=[whole(pieces.shape)],
        out_specs=whole(out),
        out_shape=jax.ShapeDtypeStruct(out, jnp.float32),
        compiler_params=PARAMS,
        name="sum_y",
    )(pieces)


def sum_z_kernel(a_ref, o_ref, g_ref):
    total = a_ref[0]
    for z in range(1, NZ):
        total = total + a_ref[z]
    for z in range(NZ):
        o_ref[z] = total[:, :RIDE]
    g_ref[...] = total[:, RIDE:]


def sum_z(pieces):
    copies, gram = (NZ, SUB, RIDE), (SUB, 2 * LANES)
    return pl.pallas_call(
        sum_z_kernel,
        grid=(1,),
        in_specs=[whole(pieces.shape)],
        out_specs=[whole(copies), whole(gram)],
        out_shape=[jax.ShapeDtypeStruct(copies, jnp.float32), jax.ShapeDtypeStruct(gram, jnp.float32)],
        compiler_params=PARAMS,
        name="sum_z",
    )(pieces)


def collect(values, axis, size):
    hops = [[(at, (at - by) % size) for at in range(size)] for by in range(1, size)]
    return jnp.concatenate([values] + [lax.ppermute(values, axis, pairs) for pairs in hops], axis=0)


def inverse_root(d):
    y = lax.rsqrt(d)
    return y * (1.5 - 0.5 * d * y * y)


def invert_factor(block, w_ref, row0, col0):
    n = LANES
    tiles = n // SUB
    a = [block[SUB * t:SUB * (t + 1)] for t in range(tiles)]
    lane = lax.broadcasted_iota(jnp.int32, (SUB, LANES), 1)
    sub = lax.broadcasted_iota(jnp.int32, (SUB, LANES), 0)
    b = [jnp.where(lane == sub + SUB * t, 1.0, 0.0).astype(jnp.float32) for t in range(tiles)]

    def across(v, j):
        return jnp.broadcast_to(v[:, j:j + 1], (SUB, LANES))

    def down(v, s):
        return jnp.broadcast_to(v[s:s + 1, :], (SUB, LANES))

    for q in range(n // 4):
        t, s, j = q // 2, (q % 2) * 4, 4 * q
        ra = [down(a[t], s + k) for k in range(4)]
        rb = [down(b[t], s + k) for k in range(4)]
        d = {}
        for x in range(4):
            for y in range(x + 1):
                d[x, y] = across(ra[y], j + x)
                d[y, x] = d[x, y]
        det = 1.0 / (d[0, 0] * d[1, 1] - d[1, 0] * d[1, 0])
        p00, p01, p11 = d[1, 1] * det, -d[1, 0] * det, d[0, 0] * det
        z = [[d[r, 0] * p00 + d[r, 1] * p01, d[r, 0] * p01 + d[r, 1] * p11] for r in (2, 3)]
        s00 = d[2, 2] - (z[0][0] * d[2, 0] + z[0][1] * d[2, 1])
        s01 = d[3, 2] - (z[1][0] * d[2, 0] + z[1][1] * d[2, 1])
        s11 = d[3, 3] - (z[1][0] * d[3, 0] + z[1][1] * d[3, 1])
        sdet = 1.0 / (s00 * s11 - s01 * s01)
        i00, i01, i11 = s11 * sdet, -s01 * sdet, s00 * sdet

        def solve(r):
            u0 = p00 * r[0] + p01 * r[1]
            u1 = p01 * r[0] + p11 * r[1]
            v2 = r[2] - (z[0][0] * r[0] + z[0][1] * r[1])
            v3 = r[3] - (z[1][0] * r[0] + z[1][1] * r[1])
            y2 = i00 * v2 + i01 * v3
            y3 = i01 * v2 + i11 * v3
            return [u0 - (z[0][0] * y2 + z[1][0] * y3), u1 - (z[0][1] * y2 + z[1][1] * y3), y2, y3]

        ya, yb = solve(ra), solve(rb)
        for u in range(t, tiles):
            if u == t and s == 4:
                continue
            c = [across(a[u], j + k) for k in range(4)]
            na, nb = a[u], b[u]
            fa = (c[0] * ya[0] + c[1] * ya[1]) + (c[2] * ya[2] + c[3] * ya[3])
            fb = (c[0] * yb[0] + c[1] * yb[1]) + (c[2] * yb[2] + c[3] * yb[3])
            if u == t:
                a[u] = jnp.where(sub >= 4, na - fa, na)
                b[u] = jnp.where(sub >= 4, nb - fb, nb)
            else:
                a[u], b[u] = na - fa, nb - fb
        k0 = inverse_root(d[0, 0])
        l10 = d[1, 0] * k0
        k1 = inverse_root(d[1, 1] - l10 * l10)
        w0 = k0 * rb[0]
        w1 = k1 * (rb[1] - l10 * w0)
        k2 = inverse_root(s00)
        l32 = s01 * k2
        k3 = inverse_root(s11 - l32 * l32)
        v2 = rb[2] - (z[0][0] * rb[0] + z[0][1] * rb[1])
        v3 = rb[3] - (z[1][0] * rb[0] + z[1][1] * rb[1])
        w2 = k2 * v2
        w3 = k3 * (v3 - l32 * w2)
        for k, w in enumerate((w0, w1, w2, w3)):
            w_ref[row0 + j + k:row0 + j + k + 1, col0:col0 + LANES] = w[0:1]


def factor_first_kernel(x_ref, y_ref, core_ref, mine_ref, other_ref, w_ref, l_ref, s_ref, g_ref):
    h = LANES
    for half, half_ref in enumerate((mine_ref, other_ref)):
        core = (core_ref[0] + half) % NC
        for dy in range(NY):
            for dx in range(NX):
                x, y = (x_ref[0] + dx) % NX, (y_ref[0] + dy) % NY
                at = pl.multiple_of(((x * NC + core) * NY + y) * SUB, SUB)
                row = (dy * NX + dx) * SUB
                g_ref[pl.ds(at, SUB), :] = half_ref[row : row + SUB, :]
    invert_factor(g_ref[:h, :h], w_ref, 0, 0)
    l21 = dot(g_ref[h:, :h], w_ref[...], NT)
    l_ref[...] = l21
    s_ref[...] = g_ref[h:, h:] - dot(l21, l21, NT)


def factor_last_kernel(w11_ref, l_ref, s_ref, p_ref, w_ref, q_ref):
    h = LANES
    w11 = w11_ref[...]
    w_ref[:h, :h] = w11
    w_ref[:h, h:] = jnp.zeros((h, h), jnp.float32)
    invert_factor(s_ref[...], w_ref, h, h)
    w_ref[h:, :h] = -dot(w_ref[h:, h:], dot(l_ref[...], w11))
    q_ref[...] = dot(p_ref[...], w_ref[...], NT)


def factor_first(mine, other):
    h, w = mine.shape
    return pl.pallas_call(
        factor_first_kernel,
        grid=(1,),
        in_specs=[SCALAR] * 3 + [whole((h, w))] * 2,
        out_specs=[whole((h, h))] * 3,
        out_shape=[jax.ShapeDtypeStruct((h, h), jnp.float32)] * 3,
        scratch_shapes=[pltpu.VMEM((w, w), jnp.float32)],
        compiler_params=PARAMS,
        name="factor_first",
    )(index_of("x"), index_of("y"), index_of("c"), mine, other)


def factor_last(w11, l21, schur, panels):
    n, w = panels.shape
    h = w // 2
    return pl.pallas_call(
        factor_last_kernel,
        grid=(1,),
        in_specs=[whole((h, h))] * 3 + [whole((n, w))],
        out_specs=[whole((w, w)), whole((n, w))],
        out_shape=[jax.ShapeDtypeStruct((w, w), jnp.float32), jax.ShapeDtypeStruct((n, w), jnp.float32)],
        compiler_params=PARAMS,
        name="factor_last",
    )(w11, l21, schur, panels)


def update_kernel(w_ref, x_ref, q_ref, c_ref, red_ref, top_ref):
    k = c_ref.shape[2]
    top = dot(w_ref[...], x_ref[...])
    fit = dot(q_ref[...], top)
    for at in range(2):
        top_ref[at] = top[:, at * k : (at + 1) * k]
        red_ref[at] = c_ref[at] - fit[:, at * k : (at + 1) * k]


def update(inverse, basis, cross, columns):
    rounds, n, k = columns.shape
    w = inverse.shape[0]
    return pl.pallas_call(
        update_kernel,
        grid=(rounds // 2,),
        in_specs=[
            pl.BlockSpec((w, w), lambda i: (0, 0)),
            pl.BlockSpec((w, 2 * k), lambda i: (0, i)),
            pl.BlockSpec((n, w), lambda i: (0, 0)),
            pl.BlockSpec((2, n, k), lambda i: (i, 0, 0)),
        ],
        out_specs=[
            pl.BlockSpec((2, n, k), lambda i: (i, 0, 0)),
            pl.BlockSpec((2, w, k), lambda i: (i, 0, 0)),
        ],
        out_shape=[
            jax.ShapeDtypeStruct((rounds, n, k), jnp.float32),
            jax.ShapeDtypeStruct((rounds, w, k), jnp.float32),
        ],
        compiler_params=PARAMS,
        name="update",
    )(inverse, cross, basis, columns)


def exchange(pieces, axis):
    return lax.all_to_all(pieces, axis, 0, 0)


def shards(matrix):
    hold = lax.optimization_barrier
    columns = jnp.transpose(matrix, (1, 0, 2))
    both, panels = products(relay(columns[0]), columns)
    w = panels.shape[1]
    pieces = sum_y(exchange(both.reshape(NY, w // NY, RIDE + LANES), "y"))
    copies, gram = sum_z(exchange(pieces, "z"))
    part = exchange(copies, "z").reshape(w // NY, RIDE)
    gram = collect(collect(gram, "x", NX), "y", NY)
    part, gram = hold((part, gram))
    inverse, basis = factor_last(*factor_first(gram, swap(gram)), panels)
    cross = exchange(jnp.broadcast_to(part[None], (NY, w // NY, RIDE)), "y").reshape(w, RIDE)
    reduced, top = update(inverse, basis, cross, columns)
    return jnp.transpose(reduced, (1, 0, 2)), jnp.transpose(top, (1, 0, 2))


def solution(mesh):
    fine = Mesh(mesh.devices.reshape(NZ, NY, NX, NC), ("z", "y", "x", "c"))
    return jax.shard_map(
        shards,
        mesh=fine,
        in_specs=(P(("z", "y"), None, ("x", "c")),),
        out_specs=(P(("z", "y"), None, ("x", "c")), P(None, None, ("x", "c"))),
        check_vma=False,
    )
```

```python
import jax
import jax.numpy as jnp
from jax import lax
from jax.experimental import pallas as pl
from jax.experimental.pallas import tpu as pltpu
from jax.sharding import Mesh, PartitionSpec as P

PRECISE = lax.Precision.HIGHEST
NZ, NY, NX, NC = 8, 4, 4, 2
LANES, SUB = 128, 8
RIDE = 1280
NT = (((1,), (1,)), ((), ()))
VMEM = pl.BlockSpec(memory_space=pltpu.VMEM)
HBM = pl.BlockSpec(memory_space=pltpu.HBM)


def in_hbm(values):
    return pltpu.with_memory_space_constraint(values, pltpu.HBM)


def params(mib):
    return pltpu.CompilerParams(vmem_limit_bytes=mib << 20)


def dot(left, right, dims=(((1,), (0,)), ((), ()))):
    return lax.dot_general(left, right, dims, precision=PRECISE, preferred_element_type=jnp.float32)


def split(values):
    high = values.astype(jnp.bfloat16)
    return high, (values - high.astype(jnp.float32)).astype(jnp.bfloat16)


def wide_left(values):
    high, low = split(values)
    return jnp.concatenate([high, high, low], axis=1)


def wide_right(values):
    high, low = split(values)
    return jnp.concatenate([high, low, high], axis=0)


def narrow_dot(left, right):
    return lax.dot_general(left, right, (((1,), (0,)), ((), ())), preferred_element_type=jnp.float32)


def pick(index, choices):
    value = choices[-1]
    for at in range(len(choices) - 2, -1, -1):
        value = jnp.where(index == at, choices[at], value)
    return value


def swap(values):
    return lax.ppermute(values, "c", [(0, 1), (1, 0)])


def relay(own):
    x = lax.axis_index("x")
    half = own.shape[0] // 2
    low, high = own[:half], own[half:]
    up_low = lax.ppermute(low, "x", [(0, 1)])
    down_high = lax.ppermute(high, "x", [(0, 3)])
    up_high = lax.ppermute(high, "x", [(0, 1)])
    down_low = lax.ppermute(low, "x", [(0, 3)])
    on_low = lax.ppermute(up_low, "x", [(1, 2)])
    on_high = lax.ppermute(down_high, "x", [(3, 2)])
    mine_low = pick(x, [low, up_low, on_low, down_low])
    mine_high = pick(x, [high, up_high, on_high, down_high])
    return mine_low, mine_high, swap(mine_low), swap(mine_high)


def index_of(axis):
    return lax.axis_index(axis).astype(jnp.int32)[None]


SCALAR = pl.BlockSpec(memory_space=pltpu.SMEM)


def place(core, pieces, p_ref):
    half, k = pieces[0].shape
    first = core == 0
    for at in range(2):
        rows = slice(at * half, (at + 1) * half)
        mine, other = pieces[at][...], pieces[2 + at][...]
        p_ref[rows, :k] = jnp.where(first, mine, other)
        p_ref[rows, k:] = jnp.where(first, other, mine)


def fetch(source, target, sem):
    copies = [pltpu.make_async_copy(source.at[r], target.at[r], sem.at[r]) for r in range(source.shape[0])]
    for copy in copies:
        copy.start()
    return copies


def products_kernel(x_ref, core_ref, ml_ref, mh_ref, ol_ref, oh_ref, c_hbm, o_ref, p_hbm, c_ref, p_ref, t_ref, sem, p_sem):
    rounds, n, k = c_ref.shape
    w = 2 * k
    arriving = fetch(c_hbm, c_ref, sem)
    place(core_ref[0], (ml_ref, mh_ref, ol_ref, oh_ref), p_ref)
    leaving = pltpu.make_async_copy(p_ref, p_hbm, p_sem)
    leaving.start()
    turned = p_ref[...].T
    t_ref[...] = turned
    left = wide_left(turned)
    share = NY * SUB
    at = pl.multiple_of((x_ref[0] * NC + core_ref[0]) * share, share)
    gram = dot(t_ref[pl.ds(at, share), :], p_ref[...])
    o_ref[:, RIDE:] = jnp.zeros((w, LANES), jnp.float32)
    for y in range(NY):
        row = y * (w // NY)
        piece = gram[y * SUB : (y + 1) * SUB]
        o_ref[row : row + SUB, RIDE:] = piece[:, :LANES]
        o_ref[row + SUB : row + 2 * SUB, RIDE:] = piece[:, LANES:]
    group = rounds // 2
    for r in range(0, rounds, group):
        for copy in arriving[r : r + group]:
            copy.wait()
        some = jnp.concatenate([c_ref[at] for at in range(r, r + group)], axis=1)
        o_ref[:, r * k : (r + group) * k] = narrow_dot(left, wide_right(some))
    leaving.wait()


def products(pieces, columns):
    rounds, n, k = columns.shape
    w = 2 * k
    return pl.pallas_call(
        products_kernel,
        in_specs=[SCALAR, SCALAR] + [VMEM] * 4 + [HBM],
        out_specs=[VMEM, HBM],
        out_shape=[
            jax.ShapeDtypeStruct((w, RIDE + LANES), jnp.float32),
            jax.ShapeDtypeStruct((n, w), jnp.float32),
        ],
        scratch_shapes=[
            pltpu.VMEM(columns.shape, jnp.float32),
            pltpu.VMEM((n, w), jnp.float32),
            pltpu.VMEM((w, n), jnp.float32),
            pltpu.SemaphoreType.DMA((rounds,)),
            pltpu.SemaphoreType.DMA(()),
        ],
        compiler_params=params(20),
        name="products",
    )(index_of("x"), index_of("c"), *pieces, columns)


def sum_y_kernel(a_ref, o_ref):
    total = (a_ref[0] + a_ref[1]) + (a_ref[2] + a_ref[3])
    for z in range(NZ):
        o_ref[z, :, :RIDE] = total[z * SUB : (z + 1) * SUB, :RIDE]
        o_ref[z, :, RIDE : RIDE + LANES] = total[:SUB, RIDE:]
        o_ref[z, :, RIDE + LANES :] = total[SUB : 2 * SUB, RIDE:]


def sum_y(pieces):
    out = (NZ, SUB, RIDE + 2 * LANES)
    return pl.pallas_call(
        sum_y_kernel,
        in_specs=[VMEM],
        out_specs=VMEM,
        out_shape=jax.ShapeDtypeStruct(out, jnp.float32),
        compiler_params=params(8),
        name="sum_y",
    )(pieces)


def total_z(a_ref, lanes):
    total = a_ref[0, :, lanes]
    for z in range(1, NZ):
        total = total + a_ref[z, :, lanes]
    return total


def copies_z_kernel(a_ref, o_ref):
    total = total_z(a_ref, slice(0, RIDE))
    for z in range(NZ):
        o_ref[z] = total


def gram_z_kernel(a_ref, o_ref):
    o_ref[...] = total_z(a_ref, slice(RIDE, RIDE + 2 * LANES))


LATE = pl.CostEstimate(flops=10**10, transcendentals=0, bytes_accessed=10**8)


def sum_z(pieces, kernel, out, name, cost=None):
    return pl.pallas_call(
        kernel,
        in_specs=[VMEM],
        out_specs=VMEM,
        out_shape=jax.ShapeDtypeStruct(out, jnp.float32),
        cost_estimate=cost,
        compiler_params=params(8),
        name=name,
    )(pieces)


def collect(values, axis, size):
    hops = [[(at, (at - by) % size) for at in range(size)] for by in range(1, size)]
    return jnp.concatenate([values] + [lax.ppermute(values, axis, pairs) for pairs in hops], axis=0)


def inverse_root(d):
    y = lax.rsqrt(d)
    return y * (1.5 - 0.5 * d * y * y)


def invert_factor(block, w_ref, row0, col0):
    n = LANES
    tiles = n // SUB
    a = [block[SUB * t:SUB * (t + 1)] for t in range(tiles)]
    lane = lax.broadcasted_iota(jnp.int32, (SUB, LANES), 1)
    sub = lax.broadcasted_iota(jnp.int32, (SUB, LANES), 0)
    b = [jnp.where(lane == sub + SUB * t, 1.0, 0.0).astype(jnp.float32) for t in range(tiles)]

    def across(v, j):
        return jnp.broadcast_to(v[:, j:j + 1], (SUB, LANES))

    def down(v, s):
        return jnp.broadcast_to(v[s:s + 1, :], (SUB, LANES))

    for q in range(n // 4):
        t, s, j = q // 2, (q % 2) * 4, 4 * q
        ra = [down(a[t], s + k) for k in range(4)]
        rb = [down(b[t], s + k) for k in range(4)]
        d = {}
        for x in range(4):
            for y in range(x + 1):
                d[x, y] = across(ra[y], j + x)
                d[y, x] = d[x, y]
        det = 1.0 / (d[0, 0] * d[1, 1] - d[1, 0] * d[1, 0])
        p00, p01, p11 = d[1, 1] * det, -d[1, 0] * det, d[0, 0] * det
        z = [[d[r, 0] * p00 + d[r, 1] * p01, d[r, 0] * p01 + d[r, 1] * p11] for r in (2, 3)]
        s00 = d[2, 2] - (z[0][0] * d[2, 0] + z[0][1] * d[2, 1])
        s01 = d[3, 2] - (z[1][0] * d[2, 0] + z[1][1] * d[2, 1])
        s11 = d[3, 3] - (z[1][0] * d[3, 0] + z[1][1] * d[3, 1])
        sdet = 1.0 / (s00 * s11 - s01 * s01)
        i00, i01, i11 = s11 * sdet, -s01 * sdet, s00 * sdet

        def solve(r):
            u0 = p00 * r[0] + p01 * r[1]
            u1 = p01 * r[0] + p11 * r[1]
            v2 = r[2] - (z[0][0] * r[0] + z[0][1] * r[1])
            v3 = r[3] - (z[1][0] * r[0] + z[1][1] * r[1])
            y2 = i00 * v2 + i01 * v3
            y3 = i01 * v2 + i11 * v3
            return [u0 - (z[0][0] * y2 + z[1][0] * y3), u1 - (z[0][1] * y2 + z[1][1] * y3), y2, y3]

        ya, yb = solve(ra), solve(rb)
        for u in range(t, tiles):
            if u == t and s == 4:
                continue
            c = [across(a[u], j + k) for k in range(4)]
            na, nb = a[u], b[u]
            fa = (c[0] * ya[0] + c[1] * ya[1]) + (c[2] * ya[2] + c[3] * ya[3])
            fb = (c[0] * yb[0] + c[1] * yb[1]) + (c[2] * yb[2] + c[3] * yb[3])
            if u == t:
                a[u] = jnp.where(sub >= 4, na - fa, na)
                b[u] = jnp.where(sub >= 4, nb - fb, nb)
            else:
                a[u], b[u] = na - fa, nb - fb
        k0 = inverse_root(d[0, 0])
        l10 = d[1, 0] * k0
        k1 = inverse_root(d[1, 1] - l10 * l10)
        w0 = k0 * rb[0]
        w1 = k1 * (rb[1] - l10 * w0)
        k2 = inverse_root(s00)
        l32 = s01 * k2
        k3 = inverse_root(s11 - l32 * l32)
        v2 = rb[2] - (z[0][0] * rb[0] + z[0][1] * rb[1])
        v3 = rb[3] - (z[1][0] * rb[0] + z[1][1] * rb[1])
        w2 = k2 * v2
        w3 = k3 * (v3 - l32 * w2)
        for k, w in enumerate((w0, w1, w2, w3)):
            w_ref[row0 + j + k:row0 + j + k + 1, col0:col0 + LANES] = w[0:1]


def factor_first_kernel(x_ref, y_ref, core_ref, mine_ref, other_ref, w_ref, l_ref, s_ref, g_ref):
    h = LANES
    for half, half_ref in enumerate((mine_ref, other_ref)):
        core = (core_ref[0] + half) % NC
        for dy in range(NY):
            for dx in range(NX):
                x, y = (x_ref[0] + dx) % NX, (y_ref[0] + dy) % NY
                at = pl.multiple_of(((x * NC + core) * NY + y) * SUB, SUB)
                row = (dy * NX + dx) * SUB
                g_ref[pl.ds(at, SUB), :] = half_ref[row : row + SUB, :]
    invert_factor(g_ref[:h, :h], w_ref, 0, 0)
    l21 = dot(g_ref[h:, :h], w_ref[...], NT)
    l_ref[...] = l21
    s_ref[...] = g_ref[h:, h:] - dot(l21, l21, NT)


def factor_last_kernel(w11_ref, l_ref, s_ref, p_hbm, w_ref, q_ref, p_ref, sem):
    arriving = pltpu.make_async_copy(p_hbm, p_ref, sem)
    arriving.start()
    h = LANES
    w11 = w11_ref[...]
    w_ref[:h, :h] = w11
    w_ref[:h, h:] = jnp.zeros((h, h), jnp.float32)
    invert_factor(s_ref[...], w_ref, h, h)
    w_ref[h:, :h] = -dot(w_ref[h:, h:], dot(l_ref[...], w11))
    arriving.wait()
    q_ref[...] = wide_left(dot(p_ref[...], w_ref[...], NT))


def factor_first(mine, other):
    h, w = mine.shape
    return pl.pallas_call(
        factor_first_kernel,
        in_specs=[SCALAR] * 3 + [VMEM] * 2,
        out_specs=[VMEM] * 3,
        out_shape=[jax.ShapeDtypeStruct((h, h), jnp.float32)] * 3,
        scratch_shapes=[pltpu.VMEM((w, w), jnp.float32)],
        compiler_params=params(8),
        name="factor_first",
    )(index_of("x"), index_of("y"), index_of("c"), mine, other)


def factor_last(w11, l21, schur, panels):
    n, w = panels.shape
    return pl.pallas_call(
        factor_last_kernel,
        in_specs=[VMEM] * 3 + [HBM],
        out_specs=[VMEM] * 2,
        out_shape=[jax.ShapeDtypeStruct((w, w), jnp.float32), jax.ShapeDtypeStruct((n, 3 * w), jnp.bfloat16)],
        scratch_shapes=[pltpu.VMEM((n, w), jnp.float32), pltpu.SemaphoreType.DMA(())],
        compiler_params=params(12),
        name="factor_last",
    )(w11, l21, schur, panels)


BAND = 256


def update_kernel(w_ref, q_ref, x_ref, c_hbm, red_hbm, top_hbm, red_ref, top_ref, c_sem, red_sem, top_sem):
    rounds, n, k = red_ref.shape
    bands = [pl.ds(at, BAND) for at in range(0, n, BAND)]
    arriving = [
        pltpu.make_async_copy(c_hbm.at[:, band], red_ref.at[:, band], c_sem.at[at]) for at, band in enumerate(bands)
    ]
    for copy in arriving:
        copy.start()
    top = narrow_dot(wide_left(w_ref[...]), wide_right(x_ref[...]))
    for r in range(rounds):
        top_ref[r] = top[:, r * k : (r + 1) * k]
    leaving = [pltpu.make_async_copy(top_ref, top_hbm, top_sem)]
    leaving[0].start()
    right = wide_right(top)
    for at, band in enumerate(bands):
        fit = narrow_dot(q_ref[at * BAND : (at + 1) * BAND], right)
        arriving[at].wait()
        for r in range(rounds):
            red_ref[r, at * BAND : (at + 1) * BAND] -= fit[:, r * k : (r + 1) * k]
        copy = pltpu.make_async_copy(red_ref.at[:, band], red_hbm.at[:, band], red_sem.at[at])
        copy.start()
        leaving.append(copy)
    for copy in leaving:
        copy.wait()


def update(inverse, basis, cross, columns):
    rounds, n, k = columns.shape
    w = inverse.shape[0]
    reduced, top = (rounds, n, k), (rounds, w, k)
    return pl.pallas_call(
        update_kernel,
        in_specs=[VMEM] * 3 + [HBM],
        out_specs=[HBM] * 2,
        out_shape=[jax.ShapeDtypeStruct(reduced, jnp.float32), jax.ShapeDtypeStruct(top, jnp.float32)],
        scratch_shapes=[
            pltpu.VMEM(reduced, jnp.float32),
            pltpu.VMEM(top, jnp.float32),
            pltpu.SemaphoreType.DMA((n // BAND,)),
            pltpu.SemaphoreType.DMA((n // BAND,)),
            pltpu.SemaphoreType.DMA(()),
        ],
        compiler_params=params(24),
        name="update",
    )(inverse, basis, cross, columns)


def exchange(pieces, axis):
    return lax.all_to_all(pieces, axis, 0, 0)


def shards(matrix):
    hold = lax.optimization_barrier
    columns = jnp.transpose(matrix, (1, 0, 2))
    own, columns = columns[0], in_hbm(columns)
    both, panels = products(relay(own), columns)
    w = panels.shape[1]
    pieces = sum_y(exchange(both.reshape(NY, w // NY, RIDE + LANES), "y"))
    pieces = exchange(pieces, "z")
    copies = sum_z(pieces, copies_z_kernel, (NZ, SUB, RIDE), "copies_z")
    copies, pieces = hold((copies, pieces))
    gram = sum_z(pieces, gram_z_kernel, (SUB, 2 * LANES), "gram_z", LATE)
    part = exchange(copies, "z").reshape(w // NY, RIDE)
    gram = collect(collect(gram, "x", NX), "y", NY)
    part, gram = hold((part, gram))
    inverse, basis = factor_last(*factor_first(gram, swap(gram)), in_hbm(panels))
    cross = exchange(jnp.broadcast_to(part[None], (NY, w // NY, RIDE)), "y").reshape(w, RIDE)
    reduced, top = update(inverse, basis, cross, columns)
    return jnp.transpose(reduced, (1, 0, 2)), jnp.transpose(top, (1, 0, 2))


def solution(mesh):
    fine = Mesh(mesh.devices.reshape(NZ, NY, NX, NC), ("z", "y", "x", "c"))
    return jax.shard_map(
        shards,
        mesh=fine,
        in_specs=(P(("z", "y"), None, ("x", "c")),),
        out_specs=(P(("z", "y"), None, ("x", "c")), P(None, None, ("x", "c"))),
        check_vma=False,
    )
```

```python
import jax
import jax.numpy as jnp
from jax import lax
from jax.experimental import pallas as pl
from jax.experimental.pallas import tpu as pltpu
from jax.sharding import Mesh, PartitionSpec as P

PRECISE = lax.Precision.HIGHEST
NZ, NY, NX, NC = 8, 4, 4, 2
LANES, SUB = 128, 8
RIDE = 1280
NT = (((1,), (1,)), ((), ()))
VMEM = pl.BlockSpec(memory_space=pltpu.VMEM)
HBM = pl.BlockSpec(memory_space=pltpu.HBM)


def in_hbm(values):
    return pltpu.with_memory_space_constraint(values, pltpu.HBM)


def params(mib):
    return pltpu.CompilerParams(vmem_limit_bytes=mib << 20)


def dot(left, right, dims=(((1,), (0,)), ((), ()))):
    return lax.dot_general(left, right, dims, precision=PRECISE, preferred_element_type=jnp.float32)


def split(values):
    high = values.astype(jnp.bfloat16)
    return high, (values - high.astype(jnp.float32)).astype(jnp.bfloat16)


def wide_left(values):
    high, low = split(values)
    return jnp.concatenate([high, high, low], axis=1)


def wide_right(values):
    high, low = split(values)
    return jnp.concatenate([high, low, high], axis=0)


def narrow_dot(left, right):
    return lax.dot_general(left, right, (((1,), (0,)), ((), ())), preferred_element_type=jnp.float32)


def pick(index, choices):
    value = choices[-1]
    for at in range(len(choices) - 2, -1, -1):
        value = jnp.where(index == at, choices[at], value)
    return value


def swap(values):
    return lax.ppermute(values, "c", [(0, 1), (1, 0)])


def relay(own):
    x = lax.axis_index("x")
    half = own.shape[0] // 2
    low, high = own[:half], own[half:]
    up_low = lax.ppermute(low, "x", [(0, 1)])
    down_high = lax.ppermute(high, "x", [(0, 3)])
    up_high = lax.ppermute(high, "x", [(0, 1)])
    down_low = lax.ppermute(low, "x", [(0, 3)])
    on_low = lax.ppermute(up_low, "x", [(1, 2)])
    on_high = lax.ppermute(down_high, "x", [(3, 2)])
    mine_low = pick(x, [low, up_low, on_low, down_low])
    mine_high = pick(x, [high, up_high, on_high, down_high])
    return mine_low, mine_high, swap(mine_low), swap(mine_high)


def index_of(axis):
    return lax.axis_index(axis).astype(jnp.int32)[None]


SCALAR = pl.BlockSpec(memory_space=pltpu.SMEM)


def place(core, pieces, p_ref):
    half, k = pieces[0].shape
    first = core == 0
    for at in range(2):
        rows = slice(at * half, (at + 1) * half)
        mine, other = pieces[at][...], pieces[2 + at][...]
        p_ref[rows, :k] = jnp.where(first, mine, other)
        p_ref[rows, k:] = jnp.where(first, other, mine)


def around(at_ref, by, size, rows, base=0):
    return pl.ds(pl.multiple_of(base + ((at_ref[0] + by) % size) * rows, SUB), rows)


def fetch(source, target, sem):
    copies = [pltpu.make_async_copy(source.at[r], target.at[r], sem.at[r]) for r in range(source.shape[0])]
    for copy in copies:
        copy.start()
    return copies


def products_kernel(
    x_ref, y_ref, core_ref, ml_ref, mh_ref, ol_ref, oh_ref, c_hbm, o0_ref, o1_ref, o2_ref, o3_ref, p_hbm, c_ref, p_ref, t_ref, sem, p_sem
):
    rounds, n, k = c_ref.shape
    w = 2 * k
    arriving = fetch(c_hbm, c_ref, sem)
    place(core_ref[0], (ml_ref, mh_ref, ol_ref, oh_ref), p_ref)
    leaving = pltpu.make_async_copy(p_ref, p_hbm, p_sem)
    leaving.start()
    t_ref[...] = p_ref[...].T
    outs = (o0_ref, o1_ref, o2_ref, o3_ref)
    part = w // NY
    left = wide_left(jnp.concatenate([t_ref[around(y_ref, by, NY, part), :] for by in range(NY)], axis=0))
    base = (x_ref[0] * NC + core_ref[0]) * (NY * SUB)
    rows = [t_ref[around(y_ref, by, NY, SUB, base), :] for by in range(NY)]
    gram = dot(jnp.concatenate(rows, axis=0), p_ref[...])
    for by, o_ref in enumerate(outs):
        piece = gram[by * SUB : (by + 1) * SUB]
        o_ref[:, RIDE:] = jnp.zeros((part, LANES), jnp.float32)
        o_ref[:SUB, RIDE:] = piece[:, :LANES]
        o_ref[SUB : 2 * SUB, RIDE:] = piece[:, LANES:]
    group = rounds // 2
    for r in range(0, rounds, group):
        for copy in arriving[r : r + group]:
            copy.wait()
        some = jnp.concatenate([c_ref[at] for at in range(r, r + group)], axis=1)
        cross = narrow_dot(left, wide_right(some))
        for by, o_ref in enumerate(outs):
            o_ref[:, r * k : (r + group) * k] = cross[by * part : (by + 1) * part]
    leaving.wait()


def products(pieces, columns):
    rounds, n, k = columns.shape
    w = 2 * k
    return pl.pallas_call(
        products_kernel,
        in_specs=[SCALAR] * 3 + [VMEM] * 4 + [HBM],
        out_specs=[VMEM] * NY + [HBM],
        out_shape=[jax.ShapeDtypeStruct((w // NY, RIDE + LANES), jnp.float32)] * NY
        + [jax.ShapeDtypeStruct((n, w), jnp.float32)],
        scratch_shapes=[
            pltpu.VMEM(columns.shape, jnp.float32),
            pltpu.VMEM((n, w), jnp.float32),
            pltpu.VMEM((w, n), jnp.float32),
            pltpu.SemaphoreType.DMA((rounds,)),
            pltpu.SemaphoreType.DMA(()),
        ],
        compiler_params=params(20),
        name="products",
    )(index_of("x"), index_of("y"), index_of("c"), *pieces, columns)


def sum_y_kernel(z_ref, *refs):
    parts, outs, t_ref = refs[:NY], refs[NY : NY + NZ], refs[-1]
    t_ref[...] = (parts[0][...] + parts[1][...]) + (parts[2][...] + parts[3][...])
    for by, o_ref in enumerate(outs):
        o_ref[:, :RIDE] = t_ref[around(z_ref, by, NZ, SUB), :RIDE]
        o_ref[:, RIDE : RIDE + LANES] = t_ref[:SUB, RIDE:]
        o_ref[:, RIDE + LANES :] = t_ref[SUB : 2 * SUB, RIDE:]


def sum_y(pieces):
    out = jax.ShapeDtypeStruct((SUB, RIDE + 2 * LANES), jnp.float32)
    return pl.pallas_call(
        sum_y_kernel,
        in_specs=[SCALAR] + [VMEM] * NY,
        out_specs=[VMEM] * NZ,
        out_shape=[out] * NZ,
        scratch_shapes=[pltpu.VMEM(pieces[0].shape, jnp.float32)],
        compiler_params=params(4),
        name="sum_y",
    )(index_of("z"), *pieces)


def sum_z_kernel(*refs):
    parts, (o_ref, g_ref) = refs[:NZ], refs[NZ:]
    total = parts[0][...]
    for part in parts[1:]:
        total = total + part[...]
    o_ref[...] = total[:, :RIDE]
    g_ref[...] = total[:, RIDE:]


def sum_z(pieces):
    return pl.pallas_call(
        sum_z_kernel,
        in_specs=[VMEM] * NZ,
        out_specs=[VMEM] * 2,
        out_shape=[
            jax.ShapeDtypeStruct((SUB, RIDE), jnp.float32),
            jax.ShapeDtypeStruct((SUB, 2 * LANES), jnp.float32),
        ],
        compiler_params=params(4),
        name="sum_z",
    )(*pieces)


def join_z_kernel(z_ref, *refs):
    for by in range(NZ):
        refs[-1][around(z_ref, by, NZ, SUB), :] = refs[by][...]


def join_z(pieces):
    return pl.pallas_call(
        join_z_kernel,
        in_specs=[SCALAR] + [VMEM] * NZ,
        out_specs=VMEM,
        out_shape=jax.ShapeDtypeStruct((NZ * SUB, RIDE), jnp.float32),
        compiler_params=params(4),
        name="join_z",
    )(index_of("z"), *pieces)


def deal(pieces, axis):
    size = len(pieces)
    return [pieces[0]] + [
        lax.ppermute(pieces[by], axis, [(at, (at + by) % size) for at in range(size)]) for by in range(1, size)
    ]


def every(values, axis, size):
    return [values] + [
        lax.ppermute(values, axis, [(at, (at - by) % size) for at in range(size)]) for by in range(1, size)
    ]


def collect(values, axis, size):
    return jnp.concatenate(every(values, axis, size), axis=0)


def inverse_root(d):
    y = lax.rsqrt(d)
    return y * (1.5 - 0.5 * d * y * y)


def invert_factor(block, w_ref, row0, col0):
    n = LANES
    tiles = n // SUB
    a = [block[SUB * t:SUB * (t + 1)] for t in range(tiles)]
    lane = lax.broadcasted_iota(jnp.int32, (SUB, LANES), 1)
    sub = lax.broadcasted_iota(jnp.int32, (SUB, LANES), 0)
    b = [jnp.where(lane == sub + SUB * t, 1.0, 0.0).astype(jnp.float32) for t in range(tiles)]

    def across(v, j):
        return jnp.broadcast_to(v[:, j:j + 1], (SUB, LANES))

    def down(v, s):
        return jnp.broadcast_to(v[s:s + 1, :], (SUB, LANES))

    for q in range(n // 4):
        t, s, j = q // 2, (q % 2) * 4, 4 * q
        ra = [down(a[t], s + k) for k in range(4)]
        rb = [down(b[t], s + k) for k in range(4)]
        d = {}
        for x in range(4):
            for y in range(x + 1):
                d[x, y] = across(ra[y], j + x)
                d[y, x] = d[x, y]
        det = 1.0 / (d[0, 0] * d[1, 1] - d[1, 0] * d[1, 0])
        p00, p01, p11 = d[1, 1] * det, -d[1, 0] * det, d[0, 0] * det
        z = [[d[r, 0] * p00 + d[r, 1] * p01, d[r, 0] * p01 + d[r, 1] * p11] for r in (2, 3)]
        s00 = d[2, 2] - (z[0][0] * d[2, 0] + z[0][1] * d[2, 1])
        s01 = d[3, 2] - (z[1][0] * d[2, 0] + z[1][1] * d[2, 1])
        s11 = d[3, 3] - (z[1][0] * d[3, 0] + z[1][1] * d[3, 1])
        sdet = 1.0 / (s00 * s11 - s01 * s01)
        i00, i01, i11 = s11 * sdet, -s01 * sdet, s00 * sdet

        def solve(r):
            u0 = p00 * r[0] + p01 * r[1]
            u1 = p01 * r[0] + p11 * r[1]
            v2 = r[2] - (z[0][0] * r[0] + z[0][1] * r[1])
            v3 = r[3] - (z[1][0] * r[0] + z[1][1] * r[1])
            y2 = i00 * v2 + i01 * v3
            y3 = i01 * v2 + i11 * v3
            return [u0 - (z[0][0] * y2 + z[1][0] * y3), u1 - (z[0][1] * y2 + z[1][1] * y3), y2, y3]

        ya, yb = solve(ra), solve(rb)
        for u in range(t, tiles):
            if u == t and s == 4:
                continue
            c = [across(a[u], j + k) for k in range(4)]
            na, nb = a[u], b[u]
            fa = (c[0] * ya[0] + c[1] * ya[1]) + (c[2] * ya[2] + c[3] * ya[3])
            fb = (c[0] * yb[0] + c[1] * yb[1]) + (c[2] * yb[2] + c[3] * yb[3])
            if u == t:
                a[u] = jnp.where(sub >= 4, na - fa, na)
                b[u] = jnp.where(sub >= 4, nb - fb, nb)
            else:
                a[u], b[u] = na - fa, nb - fb
        k0 = inverse_root(d[0, 0])
        l10 = d[1, 0] * k0
        k1 = inverse_root(d[1, 1] - l10 * l10)
        w0 = k0 * rb[0]
        w1 = k1 * (rb[1] - l10 * w0)
        k2 = inverse_root(s00)
        l32 = s01 * k2
        k3 = inverse_root(s11 - l32 * l32)
        v2 = rb[2] - (z[0][0] * rb[0] + z[0][1] * rb[1])
        v3 = rb[3] - (z[1][0] * rb[0] + z[1][1] * rb[1])
        w2 = k2 * v2
        w3 = k3 * (v3 - l32 * w2)
        for k, w in enumerate((w0, w1, w2, w3)):
            w_ref[row0 + j + k:row0 + j + k + 1, col0:col0 + LANES] = w[0:1]


def factor_first_kernel(x_ref, y_ref, core_ref, mine_ref, other_ref, w_ref, l_ref, s_ref, g_ref):
    h = LANES
    for half, half_ref in enumerate((mine_ref, other_ref)):
        core = (core_ref[0] + half) % NC
        for dy in range(NY):
            for dx in range(NX):
                x, y = (x_ref[0] + dx) % NX, (y_ref[0] + dy) % NY
                at = pl.multiple_of(((x * NC + core) * NY + y) * SUB, SUB)
                row = (dy * NX + dx) * SUB
                g_ref[pl.ds(at, SUB), :] = half_ref[row : row + SUB, :]
    invert_factor(g_ref[:h, :h], w_ref, 0, 0)
    l21 = dot(g_ref[h:, :h], w_ref[...], NT)
    l_ref[...] = l21
    s_ref[...] = g_ref[h:, h:] - dot(l21, l21, NT)


def factor_last_kernel(w11_ref, l_ref, s_ref, p_hbm, w_ref, q_ref, p_ref, sem):
    arriving = pltpu.make_async_copy(p_hbm, p_ref, sem)
    arriving.start()
    h = LANES
    w11 = w11_ref[...]
    w_ref[:h, :h] = w11
    w_ref[:h, h:] = jnp.zeros((h, h), jnp.float32)
    invert_factor(s_ref[...], w_ref, h, h)
    w_ref[h:, :h] = -dot(w_ref[h:, h:], dot(l_ref[...], w11))
    arriving.wait()
    q_ref[...] = wide_left(dot(p_ref[...], w_ref[...], NT))


def factor_first(mine, other):
    h, w = mine.shape
    return pl.pallas_call(
        factor_first_kernel,
        in_specs=[SCALAR] * 3 + [VMEM] * 2,
        out_specs=[VMEM] * 3,
        out_shape=[jax.ShapeDtypeStruct((h, h), jnp.float32)] * 3,
        scratch_shapes=[pltpu.VMEM((w, w), jnp.float32)],
        compiler_params=params(8),
        name="factor_first",
    )(index_of("x"), index_of("y"), index_of("c"), mine, other)


def factor_last(w11, l21, schur, panels):
    n, w = panels.shape
    return pl.pallas_call(
        factor_last_kernel,
        in_specs=[VMEM] * 3 + [HBM],
        out_specs=[VMEM] * 2,
        out_shape=[jax.ShapeDtypeStruct((w, w), jnp.float32), jax.ShapeDtypeStruct((n, 3 * w), jnp.bfloat16)],
        scratch_shapes=[pltpu.VMEM((n, w), jnp.float32), pltpu.SemaphoreType.DMA(())],
        compiler_params=params(12),
        name="factor_last",
    )(w11, l21, schur, panels)


BAND = 256


def update_kernel(
    y_ref, w_ref, q_ref, x0_ref, x1_ref, x2_ref, x3_ref, c_hbm, red_hbm, top_hbm, x_ref, red_ref, top_ref, c_sem, red_sem, top_sem
):
    rounds, n, k = red_ref.shape
    bands = [pl.ds(at, BAND) for at in range(0, n, BAND)]
    arriving = [
        pltpu.make_async_copy(c_hbm.at[:, band], red_ref.at[:, band], c_sem.at[at]) for at, band in enumerate(bands)
    ]
    for copy in arriving:
        copy.start()
    for by, part_ref in enumerate((x0_ref, x1_ref, x2_ref, x3_ref)):
        x_ref[around(y_ref, by, NY, part_ref.shape[0]), :] = part_ref[...]
    top = narrow_dot(wide_left(w_ref[...]), wide_right(x_ref[...]))
    for r in range(rounds):
        top_ref[r] = top[:, r * k : (r + 1) * k]
    leaving = [pltpu.make_async_copy(top_ref, top_hbm, top_sem)]
    leaving[0].start()
    right = wide_right(top)
    for at, band in enumerate(bands):
        fit = narrow_dot(q_ref[at * BAND : (at + 1) * BAND], right)
        arriving[at].wait()
        for r in range(rounds):
            red_ref[r, at * BAND : (at + 1) * BAND] -= fit[:, r * k : (r + 1) * k]
        copy = pltpu.make_async_copy(red_ref.at[:, band], red_hbm.at[:, band], red_sem.at[at])
        copy.start()
        leaving.append(copy)
    for copy in leaving:
        copy.wait()


def update(inverse, basis, cross, columns):
    rounds, n, k = columns.shape
    w = inverse.shape[0]
    reduced, top = (rounds, n, k), (rounds, w, k)
    return pl.pallas_call(
        update_kernel,
        in_specs=[SCALAR] + [VMEM] * (2 + NY) + [HBM],
        out_specs=[HBM] * 2,
        out_shape=[jax.ShapeDtypeStruct(reduced, jnp.float32), jax.ShapeDtypeStruct(top, jnp.float32)],
        scratch_shapes=[
            pltpu.VMEM((w, rounds * k), jnp.float32),
            pltpu.VMEM(reduced, jnp.float32),
            pltpu.VMEM(top, jnp.float32),
            pltpu.SemaphoreType.DMA((n // BAND,)),
            pltpu.SemaphoreType.DMA((n // BAND,)),
            pltpu.SemaphoreType.DMA(()),
        ],
        compiler_params=params(24),
        name="update",
    )(index_of("y"), inverse, basis, *cross, columns)


def shards(matrix):
    columns = jnp.transpose(matrix, (1, 0, 2))
    own, columns = columns[0], in_hbm(columns)
    *pieces, panels = products(relay(own), columns)
    part, gram = sum_z(deal(sum_y(deal(pieces, "y")), "z"))
    part = join_z(every(part, "z", NZ))
    gram = collect(collect(gram, "x", NX), "y", NY)
    part, gram = lax.optimization_barrier((part, gram))
    inverse, basis = factor_last(*factor_first(gram, swap(gram)), in_hbm(panels))
    reduced, top = update(inverse, basis, every(part, "y", NY), columns)
    return jnp.transpose(reduced, (1, 0, 2)), jnp.transpose(top, (1, 0, 2))


def solution(mesh):
    fine = Mesh(mesh.devices.reshape(NZ, NY, NX, NC), ("z", "y", "x", "c"))
    return jax.shard_map(
        shards,
        mesh=fine,
        in_specs=(P(("z", "y"), None, ("x", "c")),),
        out_specs=(P(("z", "y"), None, ("x", "c")), P(None, None, ("x", "c"))),
        check_vma=False,
    )
```

```python
import jax
import jax.numpy as jnp
from jax import lax
from jax.experimental import pallas as pl
from jax.experimental.pallas import tpu as pltpu
from jax.sharding import Mesh, PartitionSpec as P

PRECISE = lax.Precision.HIGHEST
NZ, NY, NX, NC = 8, 4, 4, 2
LANES, SUB = 128, 8
RIDE = 1280
NT = (((1,), (1,)), ((), ()))
VMEM = pl.BlockSpec(memory_space=pltpu.VMEM)
HBM = pl.BlockSpec(memory_space=pltpu.HBM)


def in_hbm(values):
    return pltpu.with_memory_space_constraint(values, pltpu.HBM)


def params(mib):
    return pltpu.CompilerParams(vmem_limit_bytes=mib << 20)


def dot(left, right, dims=(((1,), (0,)), ((), ()))):
    return lax.dot_general(left, right, dims, precision=PRECISE, preferred_element_type=jnp.float32)


def split(values):
    high = values.astype(jnp.bfloat16)
    return high, (values - high.astype(jnp.float32)).astype(jnp.bfloat16)


def wide_left(values):
    high, low = split(values)
    return jnp.concatenate([high, high, low], axis=1)


def wide_right(values):
    high, low = split(values)
    return jnp.concatenate([high, low, high], axis=0)


def narrow_dot(left, right):
    return lax.dot_general(left, right, (((1,), (0,)), ((), ())), preferred_element_type=jnp.float32)


def pick(index, choices):
    value = choices[-1]
    for at in range(len(choices) - 2, -1, -1):
        value = jnp.where(index == at, choices[at], value)
    return value


def swap(values):
    return lax.ppermute(values, "c", [(0, 1), (1, 0)])


def relay(own):
    x = lax.axis_index("x")
    half = own.shape[0] // 2
    low, high = own[:half], own[half:]
    up_low = lax.ppermute(low, "x", [(0, 1)])
    down_high = lax.ppermute(high, "x", [(0, 3)])
    up_high = lax.ppermute(high, "x", [(0, 1)])
    down_low = lax.ppermute(low, "x", [(0, 3)])
    on_low = lax.ppermute(up_low, "x", [(1, 2)])
    on_high = lax.ppermute(down_high, "x", [(3, 2)])
    mine_low = pick(x, [low, up_low, on_low, down_low])
    mine_high = pick(x, [high, up_high, on_high, down_high])
    return mine_low, mine_high, swap(mine_low), swap(mine_high)


def index_of(axis):
    return lax.axis_index(axis).astype(jnp.int32)[None]


SCALAR = pl.BlockSpec(memory_space=pltpu.SMEM)


def place(core, pieces, p_ref):
    half, k = pieces[0].shape
    first = core == 0
    for at in range(2):
        rows = slice(at * half, (at + 1) * half)
        mine, other = pieces[at][...], pieces[2 + at][...]
        p_ref[rows, :k] = jnp.where(first, mine, other)
        p_ref[rows, k:] = jnp.where(first, other, mine)


def around(at_ref, by, size, rows, base=0):
    return pl.ds(pl.multiple_of(base + ((at_ref[0] + by) % size) * rows, SUB), rows)


def fetch(source, target, sem):
    copies = [pltpu.make_async_copy(source.at[r], target.at[r], sem.at[r]) for r in range(source.shape[0])]
    for copy in copies:
        copy.start()
    return copies


def products_kernel(
    x_ref, y_ref, core_ref, ml_ref, mh_ref, ol_ref, oh_ref, c_hbm, o0_ref, o1_ref, o2_ref, o3_ref, p_hbm, c_ref, p_ref, t_ref, sem, p_sem
):
    rounds, n, k = c_ref.shape
    w = 2 * k
    arriving = fetch(c_hbm, c_ref, sem)
    place(core_ref[0], (ml_ref, mh_ref, ol_ref, oh_ref), p_ref)
    leaving = pltpu.make_async_copy(p_ref, p_hbm, p_sem)
    leaving.start()
    t_ref[...] = p_ref[...].T
    outs = (o0_ref, o1_ref, o2_ref, o3_ref)
    part = w // NY
    left = wide_left(jnp.concatenate([t_ref[around(y_ref, by, NY, part), :] for by in range(NY)], axis=0))
    base = (x_ref[0] * NC + core_ref[0]) * (NY * SUB)
    rows = [t_ref[around(y_ref, by, NY, SUB, base), :] for by in range(NY)]
    gram = dot(jnp.concatenate(rows, axis=0), p_ref[...])
    for by, o_ref in enumerate(outs):
        piece = gram[by * SUB : (by + 1) * SUB]
        o_ref[:, RIDE:] = jnp.zeros((part, LANES), jnp.float32)
        o_ref[:SUB, RIDE:] = piece[:, :LANES]
        o_ref[SUB : 2 * SUB, RIDE:] = piece[:, LANES:]
    group = rounds // 2
    for r in range(0, rounds, group):
        for copy in arriving[r : r + group]:
            copy.wait()
        some = jnp.concatenate([c_ref[at] for at in range(r, r + group)], axis=1)
        cross = narrow_dot(left, wide_right(some))
        for by, o_ref in enumerate(outs):
            o_ref[:, r * k : (r + group) * k] = cross[by * part : (by + 1) * part]
    leaving.wait()


def products(pieces, columns):
    rounds, n, k = columns.shape
    w = 2 * k
    return pl.pallas_call(
        products_kernel,
        in_specs=[SCALAR] * 3 + [VMEM] * 4 + [HBM],
        out_specs=[VMEM] * NY + [HBM],
        out_shape=[jax.ShapeDtypeStruct((w // NY, RIDE + LANES), jnp.float32)] * NY
        + [jax.ShapeDtypeStruct((n, w), jnp.float32)],
        scratch_shapes=[
            pltpu.VMEM(columns.shape, jnp.float32),
            pltpu.VMEM((n, w), jnp.float32),
            pltpu.VMEM((w, n), jnp.float32),
            pltpu.SemaphoreType.DMA((rounds,)),
            pltpu.SemaphoreType.DMA(()),
        ],
        compiler_params=params(20),
        name="products",
    )(index_of("x"), index_of("y"), index_of("c"), *pieces, columns)


def sum_y_kernel(a0_ref, a1_ref, a2_ref, a3_ref, o_ref):
    total = (a0_ref[...] + a1_ref[...]) + (a2_ref[...] + a3_ref[...])
    for z in range(NZ):
        o_ref[z, :, :RIDE] = total[z * SUB : (z + 1) * SUB, :RIDE]
        o_ref[z, :, RIDE : RIDE + LANES] = total[:SUB, RIDE:]
        o_ref[z, :, RIDE + LANES :] = total[SUB : 2 * SUB, RIDE:]


def sum_y(pieces):
    return pl.pallas_call(
        sum_y_kernel,
        in_specs=[VMEM] * NY,
        out_specs=VMEM,
        out_shape=jax.ShapeDtypeStruct((NZ, SUB, RIDE + 2 * LANES), jnp.float32),
        compiler_params=params(4),
        name="sum_y",
    )(*pieces)


def sum_z_kernel(a_ref, o_ref, g_ref):
    total = a_ref[0]
    for z in range(1, NZ):
        total = total + a_ref[z]
    for z in range(NZ):
        o_ref[z] = total[:, :RIDE]
    g_ref[...] = total[:, RIDE:]


def sum_z(pieces):
    return pl.pallas_call(
        sum_z_kernel,
        in_specs=[VMEM],
        out_specs=[VMEM] * 2,
        out_shape=[
            jax.ShapeDtypeStruct((NZ, SUB, RIDE), jnp.float32),
            jax.ShapeDtypeStruct((SUB, 2 * LANES), jnp.float32),
        ],
        compiler_params=params(4),
        name="sum_z",
    )(pieces)


def deal(pieces, axis):
    size = len(pieces)
    return [pieces[0]] + [
        lax.ppermute(pieces[by], axis, [(at, (at + by) % size) for at in range(size)]) for by in range(1, size)
    ]


def every(values, axis, size):
    return [values] + [
        lax.ppermute(values, axis, [(at, (at - by) % size) for at in range(size)]) for by in range(1, size)
    ]


def collect(values, axis, size):
    return jnp.concatenate(every(values, axis, size), axis=0)


def inverse_root(d):
    y = lax.rsqrt(d)
    return y * (1.5 - 0.5 * d * y * y)


def invert_factor(block, w_ref, row0, col0):
    n = LANES
    tiles = n // SUB
    a = [block[SUB * t:SUB * (t + 1)] for t in range(tiles)]
    lane = lax.broadcasted_iota(jnp.int32, (SUB, LANES), 1)
    sub = lax.broadcasted_iota(jnp.int32, (SUB, LANES), 0)
    b = [jnp.where(lane == sub + SUB * t, 1.0, 0.0).astype(jnp.float32) for t in range(tiles)]

    def across(v, j):
        return jnp.broadcast_to(v[:, j:j + 1], (SUB, LANES))

    def down(v, s):
        return jnp.broadcast_to(v[s:s + 1, :], (SUB, LANES))

    for q in range(n // 4):
        t, s, j = q // 2, (q % 2) * 4, 4 * q
        ra = [down(a[t], s + k) for k in range(4)]
        rb = [down(b[t], s + k) for k in range(4)]
        d = {}
        for x in range(4):
            for y in range(x + 1):
                d[x, y] = across(ra[y], j + x)
                d[y, x] = d[x, y]
        det = 1.0 / (d[0, 0] * d[1, 1] - d[1, 0] * d[1, 0])
        p00, p01, p11 = d[1, 1] * det, -d[1, 0] * det, d[0, 0] * det
        z = [[d[r, 0] * p00 + d[r, 1] * p01, d[r, 0] * p01 + d[r, 1] * p11] for r in (2, 3)]
        s00 = d[2, 2] - (z[0][0] * d[2, 0] + z[0][1] * d[2, 1])
        s01 = d[3, 2] - (z[1][0] * d[2, 0] + z[1][1] * d[2, 1])
        s11 = d[3, 3] - (z[1][0] * d[3, 0] + z[1][1] * d[3, 1])
        sdet = 1.0 / (s00 * s11 - s01 * s01)
        i00, i01, i11 = s11 * sdet, -s01 * sdet, s00 * sdet

        def solve(r):
            u0 = p00 * r[0] + p01 * r[1]
            u1 = p01 * r[0] + p11 * r[1]
            v2 = r[2] - (z[0][0] * r[0] + z[0][1] * r[1])
            v3 = r[3] - (z[1][0] * r[0] + z[1][1] * r[1])
            y2 = i00 * v2 + i01 * v3
            y3 = i01 * v2 + i11 * v3
            return [u0 - (z[0][0] * y2 + z[1][0] * y3), u1 - (z[0][1] * y2 + z[1][1] * y3), y2, y3]

        ya, yb = solve(ra), solve(rb)
        for u in range(t, tiles):
            if u == t and s == 4:
                continue
            c = [across(a[u], j + k) for k in range(4)]
            na, nb = a[u], b[u]
            fa = (c[0] * ya[0] + c[1] * ya[1]) + (c[2] * ya[2] + c[3] * ya[3])
            fb = (c[0] * yb[0] + c[1] * yb[1]) + (c[2] * yb[2] + c[3] * yb[3])
            if u == t:
                a[u] = jnp.where(sub >= 4, na - fa, na)
                b[u] = jnp.where(sub >= 4, nb - fb, nb)
            else:
                a[u], b[u] = na - fa, nb - fb
        k0 = inverse_root(d[0, 0])
        l10 = d[1, 0] * k0
        k1 = inverse_root(d[1, 1] - l10 * l10)
        w0 = k0 * rb[0]
        w1 = k1 * (rb[1] - l10 * w0)
        k2 = inverse_root(s00)
        l32 = s01 * k2
        k3 = inverse_root(s11 - l32 * l32)
        v2 = rb[2] - (z[0][0] * rb[0] + z[0][1] * rb[1])
        v3 = rb[3] - (z[1][0] * rb[0] + z[1][1] * rb[1])
        w2 = k2 * v2
        w3 = k3 * (v3 - l32 * w2)
        for k, w in enumerate((w0, w1, w2, w3)):
            w_ref[row0 + j + k:row0 + j + k + 1, col0:col0 + LANES] = w[0:1]


def factor_first_kernel(x_ref, y_ref, core_ref, mine_ref, other_ref, w_ref, l_ref, s_ref, g_ref):
    h = LANES
    for half, half_ref in enumerate((mine_ref, other_ref)):
        core = (core_ref[0] + half) % NC
        for dy in range(NY):
            for dx in range(NX):
                x, y = (x_ref[0] + dx) % NX, (y_ref[0] + dy) % NY
                at = pl.multiple_of(((x * NC + core) * NY + y) * SUB, SUB)
                row = (dy * NX + dx) * SUB
                g_ref[pl.ds(at, SUB), :] = half_ref[row : row + SUB, :]
    invert_factor(g_ref[:h, :h], w_ref, 0, 0)
    l21 = dot(g_ref[h:, :h], w_ref[...], NT)
    l_ref[...] = l21
    s_ref[...] = g_ref[h:, h:] - dot(l21, l21, NT)


def factor_last_kernel(w11_ref, l_ref, s_ref, p_hbm, w_ref, q_ref, p_ref, sem):
    arriving = pltpu.make_async_copy(p_hbm, p_ref, sem)
    arriving.start()
    h = LANES
    w11 = w11_ref[...]
    w_ref[:h, :h] = w11
    w_ref[:h, h:] = jnp.zeros((h, h), jnp.float32)
    invert_factor(s_ref[...], w_ref, h, h)
    w_ref[h:, :h] = -dot(w_ref[h:, h:], dot(l_ref[...], w11))
    arriving.wait()
    high, low = split(w_ref[...])
    right = jnp.concatenate([high, low, high], axis=1)
    basis = lax.dot_general(wide_left(p_ref[...]), right, NT, preferred_element_type=jnp.float32)
    q_ref[...] = wide_left(basis)


def factor_first(mine, other):
    h, w = mine.shape
    return pl.pallas_call(
        factor_first_kernel,
        in_specs=[SCALAR] * 3 + [VMEM] * 2,
        out_specs=[VMEM] * 3,
        out_shape=[jax.ShapeDtypeStruct((h, h), jnp.float32)] * 3,
        scratch_shapes=[pltpu.VMEM((w, w), jnp.float32)],
        compiler_params=params(8),
        name="factor_first",
    )(index_of("x"), index_of("y"), index_of("c"), mine, other)


def factor_last(w11, l21, schur, panels):
    n, w = panels.shape
    return pl.pallas_call(
        factor_last_kernel,
        in_specs=[VMEM] * 3 + [HBM],
        out_specs=[VMEM] * 2,
        out_shape=[jax.ShapeDtypeStruct((w, w), jnp.float32), jax.ShapeDtypeStruct((n, 3 * w), jnp.bfloat16)],
        scratch_shapes=[pltpu.VMEM((n, w), jnp.float32), pltpu.SemaphoreType.DMA(())],
        compiler_params=params(12),
        name="factor_last",
    )(w11, l21, schur, panels)


BAND = 256


def update_kernel(
    y_ref, w_ref, q_ref, x0_ref, x1_ref, x2_ref, x3_ref, c_hbm, red_hbm, top_hbm, x_ref, red_ref, top_ref, c_sem, red_sem, top_sem
):
    rounds, n, k = red_ref.shape
    bands = [pl.ds(at, BAND) for at in range(0, n, BAND)]
    arriving = [
        pltpu.make_async_copy(c_hbm.at[:, band], red_ref.at[:, band], c_sem.at[at]) for at, band in enumerate(bands)
    ]
    for copy in arriving:
        copy.start()
    for by, part_ref in enumerate((x0_ref, x1_ref, x2_ref, x3_ref)):
        x_ref[around(y_ref, by, NY, part_ref.shape[0]), :] = part_ref[...]
    top = narrow_dot(wide_left(w_ref[...]), wide_right(x_ref[...]))
    for r in range(rounds):
        top_ref[r] = top[:, r * k : (r + 1) * k]
    leaving = [pltpu.make_async_copy(top_ref, top_hbm, top_sem)]
    leaving[0].start()
    right = wide_right(top)
    for at, band in enumerate(bands):
        fit = narrow_dot(q_ref[at * BAND : (at + 1) * BAND], right)
        arriving[at].wait()
        for r in range(rounds):
            red_ref[r, at * BAND : (at + 1) * BAND] -= fit[:, r * k : (r + 1) * k]
        copy = pltpu.make_async_copy(red_ref.at[:, band], red_hbm.at[:, band], red_sem.at[at])
        copy.start()
        leaving.append(copy)
    for copy in leaving:
        copy.wait()


def update(inverse, basis, cross, columns):
    rounds, n, k = columns.shape
    w = inverse.shape[0]
    reduced, top = (rounds, n, k), (rounds, w, k)
    return pl.pallas_call(
        update_kernel,
        in_specs=[SCALAR] + [VMEM] * (2 + NY) + [HBM],
        out_specs=[HBM] * 2,
        out_shape=[jax.ShapeDtypeStruct(reduced, jnp.float32), jax.ShapeDtypeStruct(top, jnp.float32)],
        scratch_shapes=[
            pltpu.VMEM((w, rounds * k), jnp.float32),
            pltpu.VMEM(reduced, jnp.float32),
            pltpu.VMEM(top, jnp.float32),
            pltpu.SemaphoreType.DMA((n // BAND,)),
            pltpu.SemaphoreType.DMA((n // BAND,)),
            pltpu.SemaphoreType.DMA(()),
        ],
        compiler_params=params(24),
        name="update",
    )(index_of("y"), inverse, basis, *cross, columns)


def exchange_z(pieces):
    return lax.all_to_all(pieces, "z", 0, 0)


def shards(matrix):
    columns = jnp.transpose(matrix, (1, 0, 2))
    own, columns = columns[0], in_hbm(columns)
    *pieces, panels = products(relay(own), columns)
    copies, gram = sum_z(exchange_z(sum_y(deal(pieces, "y"))))
    part = exchange_z(copies).reshape(NZ * SUB, RIDE)
    gram = collect(collect(gram, "x", NX), "y", NY)
    part, gram = lax.optimization_barrier((part, gram))
    inverse, basis = factor_last(*factor_first(gram, swap(gram)), in_hbm(panels))
    reduced, top = update(inverse, basis, every(part, "y", NY), columns)
    return jnp.transpose(reduced, (1, 0, 2)), jnp.transpose(top, (1, 0, 2))


def solution(mesh):
    fine = Mesh(mesh.devices.reshape(NZ, NY, NX, NC), ("z", "y", "x", "c"))
    return jax.shard_map(
        shards,
        mesh=fine,
        in_specs=(P(("z", "y"), None, ("x", "c")),),
        out_specs=(P(("z", "y"), None, ("x", "c")), P(None, None, ("x", "c"))),
        check_vma=False,
    )
```

```python
import jax
import jax.numpy as jnp
from jax import lax
from jax.experimental import pallas as pl
from jax.experimental.pallas import tpu as pltpu
from jax.sharding import Mesh, PartitionSpec as P

PRECISE = lax.Precision.HIGHEST
NZ, NY, NX, NC = 8, 4, 4, 2
LANES, SUB = 128, 8
RIDE = 1280
NT = (((1,), (1,)), ((), ()))
VMEM = pl.BlockSpec(memory_space=pltpu.VMEM)
HBM = pl.BlockSpec(memory_space=pltpu.HBM)


def in_hbm(values):
    return pltpu.with_memory_space_constraint(values, pltpu.HBM)


def params(mib):
    return pltpu.CompilerParams(vmem_limit_bytes=mib << 20)


def dot(left, right, dims=(((1,), (0,)), ((), ()))):
    return lax.dot_general(left, right, dims, precision=PRECISE, preferred_element_type=jnp.float32)


def split(values):
    high = values.astype(jnp.bfloat16)
    return high, (values - high.astype(jnp.float32)).astype(jnp.bfloat16)


def wide_left(values):
    high, low = split(values)
    return jnp.concatenate([high, high, low], axis=1)


def wide_right(values):
    high, low = split(values)
    return jnp.concatenate([high, low, high], axis=0)


def narrow_dot(left, right):
    return lax.dot_general(left, right, (((1,), (0,)), ((), ())), preferred_element_type=jnp.float32)


def pick(index, choices):
    value = choices[-1]
    for at in range(len(choices) - 2, -1, -1):
        value = jnp.where(index == at, choices[at], value)
    return value


def swap(values):
    return lax.ppermute(values, "c", [(0, 1), (1, 0)])


def turned(axis, size, pairs):
    sign = [1, size - 1]
    return dict(
        axis_name=(axis, "c"),
        perm=[(a * sign[c] % size * NC + c, b * sign[c] % size * NC + c) for a, b in pairs for c in range(NC)],
    )


def relay(own):
    x = lax.axis_index("x") * jnp.where(lax.axis_index("c") == 0, 1, NX - 1) % NX
    half = own.shape[0] // 2
    low, high = own[:half], own[half:]
    up_low = lax.ppermute(low, **turned("x", NX, [(0, 1)]))
    down_high = lax.ppermute(high, **turned("x", NX, [(0, 3)]))
    up_high = lax.ppermute(high, **turned("x", NX, [(0, 1)]))
    down_low = lax.ppermute(low, **turned("x", NX, [(0, 3)]))
    on_low = lax.ppermute(up_low, **turned("x", NX, [(1, 2)]))
    on_high = lax.ppermute(down_high, **turned("x", NX, [(3, 2)]))
    mine_low = pick(x, [low, up_low, on_low, down_low])
    mine_high = pick(x, [high, up_high, on_high, down_high])
    return mine_low, mine_high, swap(mine_low), swap(mine_high)


def index_of(axis):
    return lax.axis_index(axis).astype(jnp.int32)[None]


SCALAR = pl.BlockSpec(memory_space=pltpu.SMEM)


def place(core, pieces, p_ref):
    half, k = pieces[0].shape
    first = core == 0
    for at in range(2):
        rows = slice(at * half, (at + 1) * half)
        mine, other = pieces[at][...], pieces[2 + at][...]
        p_ref[rows, :k] = jnp.where(first, mine, other)
        p_ref[rows, k:] = jnp.where(first, other, mine)


def around(y_ref, core_ref, by, rows, base=0):
    return pl.ds(pl.multiple_of(base + ((y_ref[0] + by * (1 + (NY - 2) * core_ref[0])) % NY) * rows, SUB), rows)


def fetch(source, target, sem):
    copies = [pltpu.make_async_copy(source.at[r], target.at[r], sem.at[r]) for r in range(source.shape[0])]
    for copy in copies:
        copy.start()
    return copies


def products_kernel(
    x_ref, y_ref, core_ref, ml_ref, mh_ref, ol_ref, oh_ref, c_hbm, o0_ref, o1_ref, o2_ref, o3_ref, p_hbm, c_ref, p_ref, t_ref, sem, p_sem
):
    rounds, n, k = c_ref.shape
    w = 2 * k
    arriving = fetch(c_hbm, c_ref, sem)
    place(core_ref[0], (ml_ref, mh_ref, ol_ref, oh_ref), p_ref)
    leaving = pltpu.make_async_copy(p_ref, p_hbm, p_sem)
    leaving.start()
    t_ref[...] = p_ref[...].T
    outs = (o0_ref, o1_ref, o2_ref, o3_ref)
    part = w // NY
    left = wide_left(jnp.concatenate([t_ref[around(y_ref, core_ref, by, part), :] for by in range(NY)], axis=0))
    base = (x_ref[0] * NC + core_ref[0]) * (NY * SUB)
    rows = [t_ref[around(y_ref, core_ref, by, SUB, base), :] for by in range(NY)]
    gram = dot(jnp.concatenate(rows, axis=0), p_ref[...])
    for by, o_ref in enumerate(outs):
        piece = gram[by * SUB : (by + 1) * SUB]
        o_ref[:, RIDE:] = jnp.zeros((part, LANES), jnp.float32)
        o_ref[:SUB, RIDE:] = piece[:, :LANES]
        o_ref[SUB : 2 * SUB, RIDE:] = piece[:, LANES:]
    group = rounds // 2
    for r in range(0, rounds, group):
        for copy in arriving[r : r + group]:
            copy.wait()
        some = jnp.concatenate([c_ref[at] for at in range(r, r + group)], axis=1)
        cross = narrow_dot(left, wide_right(some))
        for by, o_ref in enumerate(outs):
            o_ref[:, r * k : (r + group) * k] = cross[by * part : (by + 1) * part]
    leaving.wait()


def products(pieces, columns):
    rounds, n, k = columns.shape
    w = 2 * k
    return pl.pallas_call(
        products_kernel,
        in_specs=[SCALAR] * 3 + [VMEM] * 4 + [HBM],
        out_specs=[VMEM] * NY + [HBM],
        out_shape=[jax.ShapeDtypeStruct((w // NY, RIDE + LANES), jnp.float32)] * NY
        + [jax.ShapeDtypeStruct((n, w), jnp.float32)],
        scratch_shapes=[
            pltpu.VMEM(columns.shape, jnp.float32),
            pltpu.VMEM((n, w), jnp.float32),
            pltpu.VMEM((w, n), jnp.float32),
            pltpu.SemaphoreType.DMA((rounds,)),
            pltpu.SemaphoreType.DMA(()),
        ],
        compiler_params=params(20),
        name="products",
    )(index_of("x"), index_of("y"), index_of("c"), *pieces, columns)


def sum_y_kernel(a0_ref, a1_ref, a2_ref, a3_ref, o_ref):
    total = (a0_ref[...] + a1_ref[...]) + (a2_ref[...] + a3_ref[...])
    for z in range(NZ):
        o_ref[z, :, :RIDE] = total[z * SUB : (z + 1) * SUB, :RIDE]
        o_ref[z, :, RIDE : RIDE + LANES] = total[:SUB, RIDE:]
        o_ref[z, :, RIDE + LANES :] = total[SUB : 2 * SUB, RIDE:]


def sum_y(pieces):
    return pl.pallas_call(
        sum_y_kernel,
        in_specs=[VMEM] * NY,
        out_specs=VMEM,
        out_shape=jax.ShapeDtypeStruct((NZ, SUB, RIDE + 2 * LANES), jnp.float32),
        compiler_params=params(4),
        name="sum_y",
    )(*pieces)


def sum_z_kernel(a_ref, o_ref, g_ref):
    total = a_ref[0]
    for z in range(1, NZ):
        total = total + a_ref[z]
    for z in range(NZ):
        o_ref[z] = total[:, :RIDE]
    g_ref[...] = total[:, RIDE:]


def sum_z(pieces):
    return pl.pallas_call(
        sum_z_kernel,
        in_specs=[VMEM],
        out_specs=[VMEM] * 2,
        out_shape=[
            jax.ShapeDtypeStruct((NZ, SUB, RIDE), jnp.float32),
            jax.ShapeDtypeStruct((SUB, 2 * LANES), jnp.float32),
        ],
        compiler_params=params(4),
        name="sum_z",
    )(pieces)


def deal(pieces):
    hops = [[(y, (y + by) % NY) for y in range(NY)] for by in range(1, NY)]
    return [pieces[0]] + [lax.ppermute(piece, **turned("y", NY, pairs)) for piece, pairs in zip(pieces[1:], hops)]


def every(values):
    hops = [[(y, (y - by) % NY) for y in range(NY)] for by in range(1, NY)]
    return [values] + [lax.ppermute(values, **turned("y", NY, pairs)) for pairs in hops]


def collect(values):
    for axis in ("x", "y", "c"):
        values = lax.all_gather(values, axis, tiled=True)
    return values


def inverse_root(d):
    y = lax.rsqrt(d)
    return y * (1.5 - 0.5 * d * y * y)


def invert_factor(block, w_ref, row0, col0):
    n = LANES
    tiles = n // SUB
    a = [block[SUB * t:SUB * (t + 1)] for t in range(tiles)]
    lane = lax.broadcasted_iota(jnp.int32, (SUB, LANES), 1)
    sub = lax.broadcasted_iota(jnp.int32, (SUB, LANES), 0)
    b = [jnp.where(lane == sub + SUB * t, 1.0, 0.0).astype(jnp.float32) for t in range(tiles)]

    def across(v, j):
        return jnp.broadcast_to(v[:, j:j + 1], (SUB, LANES))

    def down(v, s):
        return jnp.broadcast_to(v[s:s + 1, :], (SUB, LANES))

    for q in range(n // 4):
        t, s, j = q // 2, (q % 2) * 4, 4 * q
        ra = [down(a[t], s + k) for k in range(4)]
        rb = [down(b[t], s + k) for k in range(4)]
        d = {}
        for x in range(4):
            for y in range(x + 1):
                d[x, y] = across(ra[y], j + x)
                d[y, x] = d[x, y]
        det = 1.0 / (d[0, 0] * d[1, 1] - d[1, 0] * d[1, 0])
        p00, p01, p11 = d[1, 1] * det, -d[1, 0] * det, d[0, 0] * det
        z = [[d[r, 0] * p00 + d[r, 1] * p01, d[r, 0] * p01 + d[r, 1] * p11] for r in (2, 3)]
        s00 = d[2, 2] - (z[0][0] * d[2, 0] + z[0][1] * d[2, 1])
        s01 = d[3, 2] - (z[1][0] * d[2, 0] + z[1][1] * d[2, 1])
        s11 = d[3, 3] - (z[1][0] * d[3, 0] + z[1][1] * d[3, 1])
        sdet = 1.0 / (s00 * s11 - s01 * s01)
        i00, i01, i11 = s11 * sdet, -s01 * sdet, s00 * sdet

        def solve(r):
            u0 = p00 * r[0] + p01 * r[1]
            u1 = p01 * r[0] + p11 * r[1]
            v2 = r[2] - (z[0][0] * r[0] + z[0][1] * r[1])
            v3 = r[3] - (z[1][0] * r[0] + z[1][1] * r[1])
            y2 = i00 * v2 + i01 * v3
            y3 = i01 * v2 + i11 * v3
            return [u0 - (z[0][0] * y2 + z[1][0] * y3), u1 - (z[0][1] * y2 + z[1][1] * y3), y2, y3]

        ya, yb = solve(ra), solve(rb)
        for u in range(t, tiles):
            if u == t and s == 4:
                continue
            c = [across(a[u], j + k) for k in range(4)]
            na, nb = a[u], b[u]
            fa = (c[0] * ya[0] + c[1] * ya[1]) + (c[2] * ya[2] + c[3] * ya[3])
            fb = (c[0] * yb[0] + c[1] * yb[1]) + (c[2] * yb[2] + c[3] * yb[3])
            if u == t:
                a[u] = jnp.where(sub >= 4, na - fa, na)
                b[u] = jnp.where(sub >= 4, nb - fb, nb)
            else:
                a[u], b[u] = na - fa, nb - fb
        k0 = inverse_root(d[0, 0])
        l10 = d[1, 0] * k0
        k1 = inverse_root(d[1, 1] - l10 * l10)
        w0 = k0 * rb[0]
        w1 = k1 * (rb[1] - l10 * w0)
        k2 = inverse_root(s00)
        l32 = s01 * k2
        k3 = inverse_root(s11 - l32 * l32)
        v2 = rb[2] - (z[0][0] * rb[0] + z[0][1] * rb[1])
        v3 = rb[3] - (z[1][0] * rb[0] + z[1][1] * rb[1])
        w2 = k2 * v2
        w3 = k3 * (v3 - l32 * w2)
        for k, w in enumerate((w0, w1, w2, w3)):
            w_ref[row0 + j + k:row0 + j + k + 1, col0:col0 + LANES] = w[0:1]


def factor_first_kernel(p_ref, w_ref, l_ref, s_ref, g_ref):
    h = LANES
    for c in range(NC):
        for y in range(NY):
            for x in range(NX):
                row, at = ((c * NY + y) * NX + x) * SUB, ((x * NC + c) * NY + y) * SUB
                g_ref[at : at + SUB, :] = p_ref[row : row + SUB, :]
    invert_factor(g_ref[:h, :h], w_ref, 0, 0)
    l21 = dot(g_ref[h:, :h], w_ref[...], NT)
    l_ref[...] = l21
    s_ref[...] = g_ref[h:, h:] - dot(l21, l21, NT)


def factor_last_kernel(w11_ref, l_ref, s_ref, p_hbm, w_ref, q_ref, p_ref, sem):
    arriving = pltpu.make_async_copy(p_hbm, p_ref, sem)
    arriving.start()
    h = LANES
    w11 = w11_ref[...]
    w_ref[:h, :h] = w11
    w_ref[:h, h:] = jnp.zeros((h, h), jnp.float32)
    invert_factor(s_ref[...], w_ref, h, h)
    w_ref[h:, :h] = -dot(w_ref[h:, h:], dot(l_ref[...], w11))
    arriving.wait()
    high, low = split(w_ref[...])
    right = jnp.concatenate([high, low, high], axis=1)
    basis = lax.dot_general(wide_left(p_ref[...]), right, NT, preferred_element_type=jnp.float32)
    q_ref[...] = wide_left(basis)


def factor_first(pieces):
    w = pieces.shape[0]
    h = w // 2
    return pl.pallas_call(
        factor_first_kernel,
        in_specs=[VMEM],
        out_specs=[VMEM] * 3,
        out_shape=[jax.ShapeDtypeStruct((h, h), jnp.float32)] * 3,
        scratch_shapes=[pltpu.VMEM((w, w), jnp.float32)],
        compiler_params=params(8),
        name="factor_first",
    )(pieces)


def factor_last(w11, l21, schur, panels):
    n, w = panels.shape
    return pl.pallas_call(
        factor_last_kernel,
        in_specs=[VMEM] * 3 + [HBM],
        out_specs=[VMEM] * 2,
        out_shape=[jax.ShapeDtypeStruct((w, w), jnp.float32), jax.ShapeDtypeStruct((n, 3 * w), jnp.bfloat16)],
        scratch_shapes=[pltpu.VMEM((n, w), jnp.float32), pltpu.SemaphoreType.DMA(())],
        compiler_params=params(12),
        name="factor_last",
    )(w11, l21, schur, panels)


BAND = 256


def update_kernel(
    y_ref, core_ref, w_ref, q_ref, x0_ref, x1_ref, x2_ref, x3_ref, c_hbm, red_hbm, top_hbm, x_ref, red_ref, top_ref, c_sem, red_sem, top_sem
):
    rounds, n, k = red_ref.shape
    bands = [pl.ds(at, BAND) for at in range(0, n, BAND)]
    arriving = [
        pltpu.make_async_copy(c_hbm.at[:, band], red_ref.at[:, band], c_sem.at[at]) for at, band in enumerate(bands)
    ]
    for copy in arriving:
        copy.start()
    for by, part_ref in enumerate((x0_ref, x1_ref, x2_ref, x3_ref)):
        x_ref[around(y_ref, core_ref, by, part_ref.shape[0]), :] = part_ref[...]
    top = narrow_dot(wide_left(w_ref[...]), wide_right(x_ref[...]))
    for r in range(rounds):
        top_ref[r] = top[:, r * k : (r + 1) * k]
    leaving = [pltpu.make_async_copy(top_ref, top_hbm, top_sem)]
    leaving[0].start()
    right = wide_right(top)
    for at, band in enumerate(bands):
        fit = narrow_dot(q_ref[at * BAND : (at + 1) * BAND], right)
        arriving[at].wait()
        for r in range(rounds):
            red_ref[r, at * BAND : (at + 1) * BAND] -= fit[:, r * k : (r + 1) * k]
        copy = pltpu.make_async_copy(red_ref.at[:, band], red_hbm.at[:, band], red_sem.at[at])
        copy.start()
        leaving.append(copy)
    for copy in leaving:
        copy.wait()


def update(inverse, basis, cross, columns):
    rounds, n, k = columns.shape
    w = inverse.shape[0]
    reduced, top = (rounds, n, k), (rounds, w, k)
    return pl.pallas_call(
        update_kernel,
        in_specs=[SCALAR] * 2 + [VMEM] * (2 + NY) + [HBM],
        out_specs=[HBM] * 2,
        out_shape=[jax.ShapeDtypeStruct(reduced, jnp.float32), jax.ShapeDtypeStruct(top, jnp.float32)],
        scratch_shapes=[
            pltpu.VMEM((w, rounds * k), jnp.float32),
            pltpu.VMEM(reduced, jnp.float32),
            pltpu.VMEM(top, jnp.float32),
            pltpu.SemaphoreType.DMA((n // BAND,)),
            pltpu.SemaphoreType.DMA((n // BAND,)),
            pltpu.SemaphoreType.DMA(()),
        ],
        compiler_params=params(24),
        name="update",
    )(index_of("y"), index_of("c"), inverse, basis, *cross, columns)


def exchange_z(pieces):
    return lax.all_to_all(pieces, "z", 0, 0)


def shards(matrix):
    columns = jnp.transpose(matrix, (1, 0, 2))
    own, columns = columns[0], in_hbm(columns)
    *pieces, panels = products(relay(own), columns)
    copies, gram = sum_z(exchange_z(sum_y(deal(pieces))))
    part = exchange_z(copies).reshape(NZ * SUB, RIDE)
    part, gram = lax.optimization_barrier((part, collect(gram)))
    inverse, basis = factor_last(*factor_first(gram), in_hbm(panels))
    reduced, top = update(inverse, basis, every(part), columns)
    return jnp.transpose(reduced, (1, 0, 2)), jnp.transpose(top, (1, 0, 2))


def solution(mesh):
    fine = Mesh(mesh.devices.reshape(NZ, NY, NX, NC), ("z", "y", "x", "c"))
    return jax.shard_map(
        shards,
        mesh=fine,
        in_specs=(P(("z", "y"), None, ("x", "c")),),
        out_specs=(P(("z", "y"), None, ("x", "c")), P(None, None, ("x", "c"))),
        check_vma=False,
    )
```

```python
import jax
import jax.numpy as jnp
from jax import lax
from jax.experimental import pallas as pl
from jax.experimental.pallas import tpu as pltpu
from jax.sharding import Mesh, PartitionSpec as P

PRECISE = lax.Precision.HIGHEST
NZ, NY, NX, NC = 8, 4, 4, 2
LANES, SUB = 128, 8
RIDE = 1280
NT = (((1,), (1,)), ((), ()))
VMEM = pl.BlockSpec(memory_space=pltpu.VMEM)
HBM = pl.BlockSpec(memory_space=pltpu.HBM)


def in_hbm(values):
    return pltpu.with_memory_space_constraint(values, pltpu.HBM)


def params(mib):
    return pltpu.CompilerParams(vmem_limit_bytes=mib << 20)


def dot(left, right, dims=(((1,), (0,)), ((), ()))):
    return lax.dot_general(left, right, dims, precision=PRECISE, preferred_element_type=jnp.float32)


def split(values):
    high = values.astype(jnp.bfloat16)
    return high, (values - high.astype(jnp.float32)).astype(jnp.bfloat16)


def wide_left(values):
    high, low = split(values)
    return jnp.concatenate([high, high, low], axis=1)


def wide_right(values):
    high, low = split(values)
    return jnp.concatenate([high, low, high], axis=0)


def narrow_dot(left, right):
    return lax.dot_general(left, right, (((1,), (0,)), ((), ())), preferred_element_type=jnp.float32)


def pick(index, choices):
    value = choices[-1]
    for at in range(len(choices) - 2, -1, -1):
        value = jnp.where(index == at, choices[at], value)
    return value


def swap(values):
    return lax.ppermute(values, "c", [(0, 1), (1, 0)])


def relay(own):
    x = lax.axis_index("x")
    half = own.shape[0] // 2
    low, high = own[:half], own[half:]
    up_low = lax.ppermute(low, "x", [(0, 1)])
    down_high = lax.ppermute(high, "x", [(0, 3)])
    up_high = lax.ppermute(high, "x", [(0, 1)])
    down_low = lax.ppermute(low, "x", [(0, 3)])
    on_low = lax.ppermute(up_low, "x", [(1, 2)])
    on_high = lax.ppermute(down_high, "x", [(3, 2)])
    mine_low = pick(x, [low, up_low, on_low, down_low])
    mine_high = pick(x, [high, up_high, on_high, down_high])
    return mine_low, mine_high, swap(mine_low), swap(mine_high)


def index_of(axis):
    return lax.axis_index(axis).astype(jnp.int32)[None]


SCALAR = pl.BlockSpec(memory_space=pltpu.SMEM)


def place(core, pieces, p_ref):
    half, k = pieces[0].shape
    first = core == 0
    for at in range(2):
        rows = slice(at * half, (at + 1) * half)
        mine, other = pieces[at][...], pieces[2 + at][...]
        p_ref[rows, :k] = jnp.where(first, mine, other)
        p_ref[rows, k:] = jnp.where(first, other, mine)


def around(at_ref, by, size, rows, base=0):
    return pl.ds(pl.multiple_of(base + ((at_ref[0] + by) % size) * rows, SUB), rows)


def fetch(source, target, sem):
    copies = [pltpu.make_async_copy(source.at[r], target.at[r], sem.at[r]) for r in range(source.shape[0])]
    for copy in copies:
        copy.start()
    return copies


def products_kernel(
    x_ref, y_ref, core_ref, ml_ref, mh_ref, ol_ref, oh_ref, c_hbm, o0_ref, o1_ref, o2_ref, o3_ref, p_hbm, c_ref, p_ref, t_ref, sem, p_sem
):
    rounds, n, k = c_ref.shape
    w = 2 * k
    arriving = fetch(c_hbm, c_ref, sem)
    place(core_ref[0], (ml_ref, mh_ref, ol_ref, oh_ref), p_ref)
    leaving = pltpu.make_async_copy(p_ref, p_hbm, p_sem)
    leaving.start()
    t_ref[...] = p_ref[...].T
    outs = (o0_ref, o1_ref, o2_ref, o3_ref)
    part = w // NY
    left = wide_left(jnp.concatenate([t_ref[around(y_ref, by, NY, part), :] for by in range(NY)], axis=0))
    base = (x_ref[0] * NC + core_ref[0]) * (NY * SUB)
    rows = [t_ref[around(y_ref, by, NY, SUB, base), :] for by in range(NY)]
    gram = dot(jnp.concatenate(rows, axis=0), p_ref[...])
    for by, o_ref in enumerate(outs):
        piece = gram[by * SUB : (by + 1) * SUB]
        o_ref[:, RIDE:] = jnp.zeros((part, LANES), jnp.float32)
        o_ref[:SUB, RIDE:] = piece[:, :LANES]
        o_ref[SUB : 2 * SUB, RIDE:] = piece[:, LANES:]
    group = rounds // 2
    for r in range(0, rounds, group):
        for copy in arriving[r : r + group]:
            copy.wait()
        some = jnp.concatenate([c_ref[at] for at in range(r, r + group)], axis=1)
        cross = narrow_dot(left, wide_right(some))
        for by, o_ref in enumerate(outs):
            o_ref[:, r * k : (r + group) * k] = cross[by * part : (by + 1) * part]
    leaving.wait()


def products(pieces, columns):
    rounds, n, k = columns.shape
    w = 2 * k
    return pl.pallas_call(
        products_kernel,
        in_specs=[SCALAR] * 3 + [VMEM] * 4 + [HBM],
        out_specs=[VMEM] * NY + [HBM],
        out_shape=[jax.ShapeDtypeStruct((w // NY, RIDE + LANES), jnp.float32)] * NY
        + [jax.ShapeDtypeStruct((n, w), jnp.float32)],
        scratch_shapes=[
            pltpu.VMEM(columns.shape, jnp.float32),
            pltpu.VMEM((n, w), jnp.float32),
            pltpu.VMEM((w, n), jnp.float32),
            pltpu.SemaphoreType.DMA((rounds,)),
            pltpu.SemaphoreType.DMA(()),
        ],
        compiler_params=params(20),
        name="products",
    )(index_of("x"), index_of("y"), index_of("c"), *pieces, columns)


def sum_y_kernel(a0_ref, a1_ref, a2_ref, a3_ref, o_ref):
    total = (a0_ref[...] + a1_ref[...]) + (a2_ref[...] + a3_ref[...])
    for z in range(NZ):
        o_ref[z, :, :RIDE] = total[z * SUB : (z + 1) * SUB, :RIDE]
        o_ref[z, :, RIDE : RIDE + LANES] = total[:SUB, RIDE:]
        o_ref[z, :, RIDE + LANES :] = total[SUB : 2 * SUB, RIDE:]


def sum_y(pieces):
    return pl.pallas_call(
        sum_y_kernel,
        in_specs=[VMEM] * NY,
        out_specs=VMEM,
        out_shape=jax.ShapeDtypeStruct((NZ, SUB, RIDE + 2 * LANES), jnp.float32),
        compiler_params=params(4),
        name="sum_y",
    )(*pieces)


def sum_z_kernel(a_ref, o_ref, g_ref):
    total = a_ref[0]
    for z in range(1, NZ):
        total = total + a_ref[z]
    for z in range(NZ):
        o_ref[z] = total[:, :RIDE]
    g_ref[...] = total[:, RIDE:]


def sum_z(pieces):
    return pl.pallas_call(
        sum_z_kernel,
        in_specs=[VMEM],
        out_specs=[VMEM] * 2,
        out_shape=[
            jax.ShapeDtypeStruct((NZ, SUB, RIDE), jnp.float32),
            jax.ShapeDtypeStruct((SUB, 2 * LANES), jnp.float32),
        ],
        compiler_params=params(4),
        name="sum_z",
    )(pieces)


def deal(pieces, axis):
    size = len(pieces)
    return [pieces[0]] + [
        lax.ppermute(pieces[by], axis, [(at, (at + by) % size) for at in range(size)]) for by in range(1, size)
    ]


def every(values, axis, size):
    return [values] + [
        lax.ppermute(values, axis, [(at, (at - by) % size) for at in range(size)]) for by in range(1, size)
    ]


def collect(values, axis, size):
    return jnp.concatenate(every(values, axis, size), axis=0)


def inverse_root(d):
    y = lax.rsqrt(d)
    return y * (1.5 - 0.5 * d * y * y)


def sum4(left, right):
    return (left[0] * right[0] + left[1] * right[1]) + (left[2] * right[2] + left[3] * right[3])


class Pivot:
    def __init__(self, d):
        det = 1.0 / (d[0][0] * d[1][1] - d[1][0] * d[1][0])
        self.p = p00, p01, p11 = d[1][1] * det, -d[1][0] * det, d[0][0] * det
        self.z = z = [[d[r][0] * p00 + d[r][1] * p01, d[r][0] * p01 + d[r][1] * p11] for r in (2, 3)]
        s00 = d[2][2] - (z[0][0] * d[2][0] + z[0][1] * d[2][1])
        s01 = d[3][2] - (z[1][0] * d[2][0] + z[1][1] * d[2][1])
        s11 = d[3][3] - (z[1][0] * d[3][0] + z[1][1] * d[3][1])
        sdet = 1.0 / (s00 * s11 - s01 * s01)
        self.i = s11 * sdet, -s01 * sdet, s00 * sdet
        self.d, self.s = d, (s00, s01, s11)

    def lower(self, r):
        z = self.z
        return [r[2 + at] - (z[at][0] * r[0] + z[at][1] * r[1]) for at in range(2)]

    def solve(self, r):
        (p00, p01, p11), (i00, i01, i11), z = self.p, self.i, self.z
        v2, v3 = self.lower(r)
        y2, y3 = i00 * v2 + i01 * v3, i01 * v2 + i11 * v3
        u0, u1 = p00 * r[0] + p01 * r[1], p01 * r[0] + p11 * r[1]
        return [u0 - (z[0][0] * y2 + z[1][0] * y3), u1 - (z[0][1] * y2 + z[1][1] * y3), y2, y3]

    def rows(self, r):
        d, (s00, s01, s11) = self.d, self.s
        k0 = inverse_root(d[0][0])
        l10 = d[1][0] * k0
        w0 = k0 * r[0]
        w1 = inverse_root(d[1][1] - l10 * l10) * (r[1] - l10 * w0)
        k2 = inverse_root(s00)
        l32 = s01 * k2
        v2, v3 = self.lower(r)
        w2 = k2 * v2
        return [w0, w1, w2, inverse_root(s11 - l32 * l32) * (v3 - l32 * w2)]


def invert_factor(block, w_ref, row0, col0):
    n = LANES
    tiles = n // SUB
    a = [block[SUB * t : SUB * (t + 1)] for t in range(tiles)]
    lane = lax.broadcasted_iota(jnp.int32, (SUB, LANES), 1)
    sub = lax.broadcasted_iota(jnp.int32, (SUB, LANES), 0)
    b = [jnp.where(lane == sub + SUB * t, 1.0, 0.0).astype(jnp.float32) for t in range(tiles)]

    def across(v, j):
        return jnp.broadcast_to(v[:, j : j + 1], (SUB, LANES))

    def down(v, s):
        return jnp.broadcast_to(v[s : s + 1, :], (SUB, LANES))

    for t in range(tiles):
        j = SUB * t
        columns = [across(a[t], j + k) for k in range(SUB)]
        d = [[down(columns[y], x) for y in range(SUB)] for x in range(SUB)]
        ra = [down(a[t], k) for k in range(SUB)]
        rb = [down(b[t], k) for k in range(SUB)]
        head = Pivot([row[:4] for row in d[:4]])
        g = [head.solve([d[y][k] for k in range(4)]) for y in range(4, SUB)]
        rest = [[None] * 4 for _ in range(4)]
        for x in range(4):
            for y in range(x + 1):
                rest[x][y] = rest[y][x] = d[4 + x][4 + y] - sum4(d[4 + x][:4], g[y])
        tail = Pivot(rest)
        za, zb, low_b = [], [], None
        for r, z in ((ra, za), (rb, zb)):
            low = [r[4 + x] - sum4(g[x], r[:4]) for x in range(4)]
            y1, y2 = head.solve(r[:4]), tail.solve(low)
            z += [y1[k] - sum4([g[x][k] for x in range(4)], y2) for k in range(4)] + y2
            low_b = low
        for u in range(t + 1, tiles):
            c = [across(a[u], j + k) for k in range(SUB)]
            a[u], b[u] = (
                v - (sum4(c[:4], z[:4]) + sum4(c[4:], z[4:])) for v, z in ((a[u], za), (b[u], zb))
            )
        for k, w in enumerate(head.rows(rb[:4]) + tail.rows(low_b)):
            w_ref[row0 + j + k : row0 + j + k + 1, col0 : col0 + LANES] = w[0:1]


def factor_first_kernel(x_ref, y_ref, core_ref, mine_ref, other_ref, w_ref, l_ref, s_ref, g_ref):
    h = LANES
    for half, half_ref in enumerate((mine_ref, other_ref)):
        core = (core_ref[0] + half) % NC
        for dy in range(NY):
            for dx in range(NX):
                x, y = (x_ref[0] + dx) % NX, (y_ref[0] + dy) % NY
                at = pl.multiple_of(((x * NC + core) * NY + y) * SUB, SUB)
                row = (dy * NX + dx) * SUB
                g_ref[pl.ds(at, SUB), :] = half_ref[row : row + SUB, :]
    invert_factor(g_ref[:h, :h], w_ref, 0, 0)
    l21 = dot(g_ref[h:, :h], w_ref[...], NT)
    l_ref[...] = l21
    s_ref[...] = g_ref[h:, h:] - dot(l21, l21, NT)


def factor_last_kernel(w11_ref, l_ref, s_ref, p_hbm, w_ref, q_ref, p_ref, sem):
    arriving = pltpu.make_async_copy(p_hbm, p_ref, sem)
    arriving.start()
    h = LANES
    w11 = w11_ref[...]
    w_ref[:h, :h] = w11
    w_ref[:h, h:] = jnp.zeros((h, h), jnp.float32)
    invert_factor(s_ref[...], w_ref, h, h)
    w_ref[h:, :h] = -dot(w_ref[h:, h:], dot(l_ref[...], w11))
    arriving.wait()
    high, low = split(w_ref[...])
    right = jnp.concatenate([high, low, high], axis=1)
    basis = lax.dot_general(wide_left(p_ref[...]), right, NT, preferred_element_type=jnp.float32)
    q_ref[...] = wide_left(basis)


def factor_first(mine, other):
    h, w = mine.shape
    return pl.pallas_call(
        factor_first_kernel,
        in_specs=[SCALAR] * 3 + [VMEM] * 2,
        out_specs=[VMEM] * 3,
        out_shape=[jax.ShapeDtypeStruct((h, h), jnp.float32)] * 3,
        scratch_shapes=[pltpu.VMEM((w, w), jnp.float32)],
        compiler_params=params(8),
        name="factor_first",
    )(index_of("x"), index_of("y"), index_of("c"), mine, other)


def factor_last(w11, l21, schur, panels):
    n, w = panels.shape
    return pl.pallas_call(
        factor_last_kernel,
        in_specs=[VMEM] * 3 + [HBM],
        out_specs=[VMEM] * 2,
        out_shape=[jax.ShapeDtypeStruct((w, w), jnp.float32), jax.ShapeDtypeStruct((n, 3 * w), jnp.bfloat16)],
        scratch_shapes=[pltpu.VMEM((n, w), jnp.float32), pltpu.SemaphoreType.DMA(())],
        compiler_params=params(12),
        name="factor_last",
    )(w11, l21, schur, panels)


BAND = 256


def update_kernel(
    y_ref, w_ref, q_ref, x0_ref, x1_ref, x2_ref, x3_ref, c_hbm, red_hbm, top_hbm, x_ref, red_ref, top_ref, c_sem, red_sem, top_sem
):
    rounds, n, k = red_ref.shape
    bands = [pl.ds(at, BAND) for at in range(0, n, BAND)]
    arriving = [
        pltpu.make_async_copy(c_hbm.at[:, band], red_ref.at[:, band], c_sem.at[at]) for at, band in enumerate(bands)
    ]
    for copy in arriving:
        copy.start()
    for by, part_ref in enumerate((x0_ref, x1_ref, x2_ref, x3_ref)):
        x_ref[around(y_ref, by, NY, part_ref.shape[0]), :] = part_ref[...]
    top = narrow_dot(wide_left(w_ref[...]), wide_right(x_ref[...]))
    for r in range(rounds):
        top_ref[r] = top[:, r * k : (r + 1) * k]
    leaving = [pltpu.make_async_copy(top_ref, top_hbm, top_sem)]
    leaving[0].start()
    right = wide_right(top)
    for at, band in enumerate(bands):
        fit = narrow_dot(q_ref[at * BAND : (at + 1) * BAND], right)
        arriving[at].wait()
        for r in range(rounds):
            red_ref[r, at * BAND : (at + 1) * BAND] -= fit[:, r * k : (r + 1) * k]
        copy = pltpu.make_async_copy(red_ref.at[:, band], red_hbm.at[:, band], red_sem.at[at])
        copy.start()
        leaving.append(copy)
    for copy in leaving:
        copy.wait()


def update(inverse, basis, cross, columns):
    rounds, n, k = columns.shape
    w = inverse.shape[0]
    reduced, top = (rounds, n, k), (rounds, w, k)
    return pl.pallas_call(
        update_kernel,
        in_specs=[SCALAR] + [VMEM] * (2 + NY) + [HBM],
        out_specs=[HBM] * 2,
        out_shape=[jax.ShapeDtypeStruct(reduced, jnp.float32), jax.ShapeDtypeStruct(top, jnp.float32)],
        scratch_shapes=[
            pltpu.VMEM((w, rounds * k), jnp.float32),
            pltpu.VMEM(reduced, jnp.float32),
            pltpu.VMEM(top, jnp.float32),
            pltpu.SemaphoreType.DMA((n // BAND,)),
            pltpu.SemaphoreType.DMA((n // BAND,)),
            pltpu.SemaphoreType.DMA(()),
        ],
        compiler_params=params(24),
        name="update",
    )(index_of("y"), inverse, basis, *cross, columns)


def exchange_z(pieces):
    return lax.all_to_all(pieces, "z", 0, 0)


def shards(matrix):
    columns = jnp.transpose(matrix, (1, 0, 2))
    own, columns = columns[0], in_hbm(columns)
    *pieces, panels = products(relay(own), columns)
    copies, gram = sum_z(exchange_z(sum_y(deal(pieces, "y"))))
    part = exchange_z(copies).reshape(NZ * SUB, RIDE)
    gram = collect(collect(gram, "x", NX), "y", NY)
    part, gram = lax.optimization_barrier((part, gram))
    inverse, basis = factor_last(*factor_first(gram, swap(gram)), in_hbm(panels))
    reduced, top = update(inverse, basis, every(part, "y", NY), columns)
    return jnp.transpose(reduced, (1, 0, 2)), jnp.transpose(top, (1, 0, 2))


def solution(mesh):
    fine = Mesh(mesh.devices.reshape(NZ, NY, NX, NC), ("z", "y", "x", "c"))
    return jax.shard_map(
        shards,
        mesh=fine,
        in_specs=(P(("z", "y"), None, ("x", "c")),),
        out_specs=(P(("z", "y"), None, ("x", "c")), P(None, None, ("x", "c"))),
        check_vma=False,
    )
```

```python
import jax
import jax.numpy as jnp
from jax import lax
from jax.experimental import pallas as pl
from jax.experimental.pallas import tpu as pltpu
from jax.sharding import Mesh, PartitionSpec as P

PRECISE = lax.Precision.HIGHEST
NZ, NY, NX, NC = 8, 4, 4, 2
LANES, SUB = 128, 8
RIDE = 1280
NT = (((1,), (1,)), ((), ()))
VMEM = pl.BlockSpec(memory_space=pltpu.VMEM)
HBM = pl.BlockSpec(memory_space=pltpu.HBM)


def in_hbm(values):
    return pltpu.with_memory_space_constraint(values, pltpu.HBM)


def params(mib):
    return pltpu.CompilerParams(vmem_limit_bytes=mib << 20)


def dot(left, right, dims=(((1,), (0,)), ((), ()))):
    return lax.dot_general(left, right, dims, precision=PRECISE, preferred_element_type=jnp.float32)


def split(values):
    high = values.astype(jnp.bfloat16)
    return high, (values - high.astype(jnp.float32)).astype(jnp.bfloat16)


def wide_left(values):
    high, low = split(values)
    return jnp.concatenate([high, high, low], axis=1)


def wide_right(values):
    high, low = split(values)
    return jnp.concatenate([high, low, high], axis=0)


def narrow_dot(left, right):
    return lax.dot_general(left, right, (((1,), (0,)), ((), ())), preferred_element_type=jnp.float32)


def pick(index, choices):
    value = choices[-1]
    for at in range(len(choices) - 2, -1, -1):
        value = jnp.where(index == at, choices[at], value)
    return value


def swap(values):
    return lax.ppermute(values, "c", [(0, 1), (1, 0)])


def relay(own):
    x = lax.axis_index("x")
    half = own.shape[0] // 2
    low, high = own[:half], own[half:]
    up_low = lax.ppermute(low, "x", [(0, 1)])
    down_high = lax.ppermute(high, "x", [(0, 3)])
    up_high = lax.ppermute(high, "x", [(0, 1)])
    down_low = lax.ppermute(low, "x", [(0, 3)])
    on_low = lax.ppermute(up_low, "x", [(1, 2)])
    on_high = lax.ppermute(down_high, "x", [(3, 2)])
    mine_low = pick(x, [low, up_low, on_low, down_low])
    mine_high = pick(x, [high, up_high, on_high, down_high])
    return mine_low, mine_high, swap(mine_low), swap(mine_high)


def index_of(axis):
    return lax.axis_index(axis).astype(jnp.int32)[None]


SCALAR = pl.BlockSpec(memory_space=pltpu.SMEM)


def place(core, pieces, p_ref):
    half, k = pieces[0].shape
    first = core == 0
    for at in range(2):
        rows = slice(at * half, (at + 1) * half)
        mine, other = pieces[at][...], pieces[2 + at][...]
        p_ref[rows, :k] = jnp.where(first, mine, other)
        p_ref[rows, k:] = jnp.where(first, other, mine)


def around(at_ref, by, size, rows, base=0):
    return pl.ds(pl.multiple_of(base + ((at_ref[0] + by) % size) * rows, SUB), rows)


def fetch(source, target, sem):
    copies = [pltpu.make_async_copy(source.at[r], target.at[r], sem.at[r]) for r in range(source.shape[0])]
    for copy in copies:
        copy.start()
    return copies


def products_kernel(
    x_ref, y_ref, core_ref, ml_ref, mh_ref, ol_ref, oh_ref, c_hbm, o0_ref, o1_ref, o2_ref, o3_ref, p_hbm, c_ref, p_ref, t_ref, sem, p_sem
):
    rounds, n, k = c_ref.shape
    w = 2 * k
    arriving = fetch(c_hbm, c_ref, sem)
    place(core_ref[0], (ml_ref, mh_ref, ol_ref, oh_ref), p_ref)
    leaving = pltpu.make_async_copy(p_ref, p_hbm, p_sem)
    leaving.start()
    t_ref[...] = p_ref[...].T
    outs = (o0_ref, o1_ref, o2_ref, o3_ref)
    part = w // NY
    left = wide_left(jnp.concatenate([t_ref[around(y_ref, by, NY, part), :] for by in range(NY)], axis=0))
    base = (x_ref[0] * NC + core_ref[0]) * (NY * SUB)
    rows = [t_ref[around(y_ref, by, NY, SUB, base), :] for by in range(NY)]
    gram = dot(jnp.concatenate(rows, axis=0), p_ref[...])
    for by, o_ref in enumerate(outs):
        piece = gram[by * SUB : (by + 1) * SUB]
        o_ref[:, RIDE:] = jnp.zeros((part, LANES), jnp.float32)
        o_ref[:SUB, RIDE:] = piece[:, :LANES]
        o_ref[SUB : 2 * SUB, RIDE:] = piece[:, LANES:]
    group = rounds // 2
    for r in range(0, rounds, group):
        for copy in arriving[r : r + group]:
            copy.wait()
        some = jnp.concatenate([c_ref[at] for at in range(r, r + group)], axis=1)
        cross = narrow_dot(left, wide_right(some))
        for by, o_ref in enumerate(outs):
            o_ref[:, r * k : (r + group) * k] = cross[by * part : (by + 1) * part]
    leaving.wait()


def products(pieces, columns):
    rounds, n, k = columns.shape
    w = 2 * k
    return pl.pallas_call(
        products_kernel,
        in_specs=[SCALAR] * 3 + [VMEM] * 4 + [HBM],
        out_specs=[VMEM] * NY + [HBM],
        out_shape=[jax.ShapeDtypeStruct((w // NY, RIDE + LANES), jnp.float32)] * NY
        + [jax.ShapeDtypeStruct((n, w), jnp.float32)],
        scratch_shapes=[
            pltpu.VMEM(columns.shape, jnp.float32),
            pltpu.VMEM((n, w), jnp.float32),
            pltpu.VMEM((w, n), jnp.float32),
            pltpu.SemaphoreType.DMA((rounds,)),
            pltpu.SemaphoreType.DMA(()),
        ],
        compiler_params=params(20),
        name="products",
    )(index_of("x"), index_of("y"), index_of("c"), *pieces, columns)


def sum_y_kernel(a0_ref, a1_ref, a2_ref, a3_ref, o_ref):
    total = (a0_ref[...] + a1_ref[...]) + (a2_ref[...] + a3_ref[...])
    for z in range(NZ):
        o_ref[z, :, :RIDE] = total[z * SUB : (z + 1) * SUB, :RIDE]
        o_ref[z, :, RIDE : RIDE + LANES] = total[:SUB, RIDE:]
        o_ref[z, :, RIDE + LANES :] = total[SUB : 2 * SUB, RIDE:]


def sum_y(pieces):
    return pl.pallas_call(
        sum_y_kernel,
        in_specs=[VMEM] * NY,
        out_specs=VMEM,
        out_shape=jax.ShapeDtypeStruct((NZ, SUB, RIDE + 2 * LANES), jnp.float32),
        compiler_params=params(4),
        name="sum_y",
    )(*pieces)


def sum_z_kernel(a_ref, o_ref, g_ref):
    total = a_ref[0]
    for z in range(1, NZ):
        total = total + a_ref[z]
    for z in range(NZ):
        o_ref[z] = total[:, :RIDE]
    g_ref[...] = total[:, RIDE:]


def sum_z(pieces):
    return pl.pallas_call(
        sum_z_kernel,
        in_specs=[VMEM],
        out_specs=[VMEM] * 2,
        out_shape=[
            jax.ShapeDtypeStruct((NZ, SUB, RIDE), jnp.float32),
            jax.ShapeDtypeStruct((SUB, 2 * LANES), jnp.float32),
        ],
        compiler_params=params(4),
        name="sum_z",
    )(pieces)


def deal(pieces, axis):
    size = len(pieces)
    return [pieces[0]] + [
        lax.ppermute(pieces[by], axis, [(at, (at + by) % size) for at in range(size)]) for by in range(1, size)
    ]


def every(values, axis, size):
    return [values] + [
        lax.ppermute(values, axis, [(at, (at - by) % size) for at in range(size)]) for by in range(1, size)
    ]


def collect(values, axis, size):
    return jnp.concatenate(every(values, axis, size), axis=0)


def inverse_root(d):
    y = lax.rsqrt(d)
    return y * (1.5 - 0.5 * d * y * y)


def sum4(left, right):
    return (left[0] * right[0] + left[1] * right[1]) + (left[2] * right[2] + left[3] * right[3])


class Pivot:
    def __init__(self, d):
        det = 1.0 / (d[0][0] * d[1][1] - d[1][0] * d[1][0])
        self.p = p00, p01, p11 = d[1][1] * det, -d[1][0] * det, d[0][0] * det
        self.z = z = [[d[r][0] * p00 + d[r][1] * p01, d[r][0] * p01 + d[r][1] * p11] for r in (2, 3)]
        s00 = d[2][2] - (z[0][0] * d[2][0] + z[0][1] * d[2][1])
        s01 = d[3][2] - (z[1][0] * d[2][0] + z[1][1] * d[2][1])
        s11 = d[3][3] - (z[1][0] * d[3][0] + z[1][1] * d[3][1])
        sdet = 1.0 / (s00 * s11 - s01 * s01)
        self.i = s11 * sdet, -s01 * sdet, s00 * sdet
        self.d, self.s = d, (s00, s01, s11)

    def lower(self, r):
        z = self.z
        return [r[2 + at] - (z[at][0] * r[0] + z[at][1] * r[1]) for at in range(2)]

    def solve(self, r):
        (p00, p01, p11), (i00, i01, i11), z = self.p, self.i, self.z
        v2, v3 = self.lower(r)
        y2, y3 = i00 * v2 + i01 * v3, i01 * v2 + i11 * v3
        u0, u1 = p00 * r[0] + p01 * r[1], p01 * r[0] + p11 * r[1]
        return [u0 - (z[0][0] * y2 + z[1][0] * y3), u1 - (z[0][1] * y2 + z[1][1] * y3), y2, y3]

    def rows(self, r):
        d, (s00, s01, s11) = self.d, self.s
        k0 = inverse_root(d[0][0])
        l10 = d[1][0] * k0
        w0 = k0 * r[0]
        w1 = inverse_root(d[1][1] - l10 * l10) * (r[1] - l10 * w0)
        k2 = inverse_root(s00)
        l32 = s01 * k2
        v2, v3 = self.lower(r)
        w2 = k2 * v2
        return [w0, w1, w2, inverse_root(s11 - l32 * l32) * (v3 - l32 * w2)]


def invert_factor(block, w_ref, row0, col0):
    n = LANES
    tiles = n // SUB
    a = [block[SUB * t : SUB * (t + 1)] for t in range(tiles)]
    lane = lax.broadcasted_iota(jnp.int32, (SUB, LANES), 1)
    sub = lax.broadcasted_iota(jnp.int32, (SUB, LANES), 0)
    b = [jnp.where(lane == sub + SUB * t, 1.0, 0.0).astype(jnp.float32) for t in range(tiles)]

    def across(v, j):
        return jnp.broadcast_to(v[:, j : j + 1], (SUB, LANES))

    def down(v, s):
        return jnp.broadcast_to(v[s : s + 1, :], (SUB, LANES))

    for t in range(tiles):
        j = SUB * t
        columns = [across(a[t], j + k) for k in range(SUB)]
        d = [[down(columns[y], x) for y in range(SUB)] for x in range(SUB)]
        ra = [down(a[t], k) for k in range(SUB)]
        rb = [down(b[t], k) for k in range(SUB)]
        head = Pivot([row[:4] for row in d[:4]])
        g = [head.solve([d[y][k] for k in range(4)]) for y in range(4, SUB)]
        rest = [[None] * 4 for _ in range(4)]
        for x in range(4):
            for y in range(x + 1):
                rest[x][y] = rest[y][x] = d[4 + x][4 + y] - sum4(d[4 + x][:4], g[y])
        tail = Pivot(rest)
        za, zb, low_b = [], [], None
        for r, z in ((ra, za), (rb, zb)):
            low = [r[4 + x] - sum4(g[x], r[:4]) for x in range(4)]
            y1, y2 = head.solve(r[:4]), tail.solve(low)
            z += [y1[k] - sum4([g[x][k] for x in range(4)], y2) for k in range(4)] + y2
            low_b = low
        for u in range(t + 1, tiles):
            c = [across(a[u], j + k) for k in range(SUB)]
            a[u], b[u] = (
                v - (sum4(c[:4], z[:4]) + sum4(c[4:], z[4:])) for v, z in ((a[u], za), (b[u], zb))
            )
        for k, w in enumerate(head.rows(rb[:4]) + tail.rows(low_b)):
            w_ref[row0 + j + k : row0 + j + k + 1, col0 : col0 + LANES] = w[0:1]


def factor_first_kernel(x_ref, y_ref, core_ref, p_ref, w_ref, l_ref, s_ref, g_ref):
    h = LANES
    for dy in range(NY):
        for dx in range(NX):
            for dc in range(NC):
                x, y, core = (x_ref[0] + dx) % NX, (y_ref[0] + dy) % NY, (core_ref[0] + dc) % NC
                at = pl.multiple_of(((x * NC + core) * NY + y) * SUB, SUB)
                row = ((dy * NX + dx) * NC + dc) * SUB
                g_ref[pl.ds(at, SUB), :] = p_ref[row : row + SUB, :]
    invert_factor(g_ref[:h, :h], w_ref, 0, 0)
    l21 = dot(g_ref[h:, :h], w_ref[...], NT)
    l_ref[...] = l21
    s_ref[...] = g_ref[h:, h:] - dot(l21, l21, NT)


def factor_last_kernel(w11_ref, l_ref, s_ref, p_hbm, c_hbm, w_ref, q_ref, c_ref, p_ref, sem, c_sem):
    arriving = pltpu.make_async_copy(p_hbm, p_ref, sem)
    arriving.start()
    resident = pltpu.make_async_copy(c_hbm, c_ref, c_sem)
    resident.start()
    h = LANES
    w11 = w11_ref[...]
    w_ref[:h, :h] = w11
    w_ref[:h, h:] = jnp.zeros((h, h), jnp.float32)
    invert_factor(s_ref[...], w_ref, h, h)
    w_ref[h:, :h] = -dot(w_ref[h:, h:], dot(l_ref[...], w11))
    arriving.wait()
    high, low = split(w_ref[...])
    right = jnp.concatenate([high, low, high], axis=1)
    basis = lax.dot_general(wide_left(p_ref[...]), right, NT, preferred_element_type=jnp.float32)
    q_ref[...] = wide_left(basis)
    resident.wait()


def factor_first(pieces):
    w = pieces.shape[0]
    h = w // 2
    return pl.pallas_call(
        factor_first_kernel,
        in_specs=[SCALAR] * 3 + [VMEM],
        out_specs=[VMEM] * 3,
        out_shape=[jax.ShapeDtypeStruct((h, h), jnp.float32)] * 3,
        scratch_shapes=[pltpu.VMEM((w, w), jnp.float32)],
        compiler_params=params(8),
        name="factor_first",
    )(index_of("x"), index_of("y"), index_of("c"), pieces)


def factor_last(w11, l21, schur, panels, columns):
    n, w = panels.shape
    return pl.pallas_call(
        factor_last_kernel,
        in_specs=[VMEM] * 3 + [HBM] * 2,
        out_specs=[VMEM] * 3,
        out_shape=[
            jax.ShapeDtypeStruct((w, w), jnp.float32),
            jax.ShapeDtypeStruct((n, 3 * w), jnp.bfloat16),
            jax.ShapeDtypeStruct(columns.shape, jnp.float32),
        ],
        scratch_shapes=[
            pltpu.VMEM((n, w), jnp.float32),
            pltpu.SemaphoreType.DMA(()),
            pltpu.SemaphoreType.DMA(()),
        ],
        compiler_params=params(12),
        name="factor_last",
    )(w11, l21, schur, panels, columns)


BAND = 256


def update_kernel(
    y_ref, w_ref, q_ref, x0_ref, x1_ref, x2_ref, x3_ref, c_ref, red_hbm, top_hbm, x_ref, red_ref, top_ref, red_sem, top_sem
):
    rounds, n, k = red_ref.shape
    bands = [pl.ds(at, BAND) for at in range(0, n, BAND)]
    for by, part_ref in enumerate((x0_ref, x1_ref, x2_ref, x3_ref)):
        x_ref[around(y_ref, by, NY, part_ref.shape[0]), :] = part_ref[...]
    top = narrow_dot(wide_left(w_ref[...]), wide_right(x_ref[...]))
    for r in range(rounds):
        top_ref[r] = top[:, r * k : (r + 1) * k]
    leaving = [pltpu.make_async_copy(top_ref, top_hbm, top_sem)]
    leaving[0].start()
    right = wide_right(top)
    for at, band in enumerate(bands):
        fit = narrow_dot(q_ref[at * BAND : (at + 1) * BAND], right)
        rows = slice(at * BAND, (at + 1) * BAND)
        for r in range(rounds):
            red_ref[r, rows] = c_ref[r, rows] - fit[:, r * k : (r + 1) * k]
        copy = pltpu.make_async_copy(red_ref.at[:, band], red_hbm.at[:, band], red_sem.at[at])
        copy.start()
        leaving.append(copy)
    for copy in leaving:
        copy.wait()


def update(inverse, basis, cross, columns):
    rounds, n, k = columns.shape
    w = inverse.shape[0]
    reduced, top = (rounds, n, k), (rounds, w, k)
    return pl.pallas_call(
        update_kernel,
        in_specs=[SCALAR] + [VMEM] * (3 + NY),
        out_specs=[HBM] * 2,
        out_shape=[jax.ShapeDtypeStruct(reduced, jnp.float32), jax.ShapeDtypeStruct(top, jnp.float32)],
        scratch_shapes=[
            pltpu.VMEM((w, rounds * k), jnp.float32),
            pltpu.VMEM(reduced, jnp.float32),
            pltpu.VMEM(top, jnp.float32),
            pltpu.SemaphoreType.DMA((n // BAND,)),
            pltpu.SemaphoreType.DMA(()),
        ],
        compiler_params=params(24),
        name="update",
    )(index_of("y"), inverse, basis, *cross, columns)


def exchange_z(pieces):
    return lax.all_to_all(pieces, "z", 0, 0)


def shards(matrix):
    columns = jnp.transpose(matrix, (1, 0, 2))
    own, columns = columns[0], in_hbm(columns)
    *pieces, panels = products(relay(own), columns)
    copies, gram = sum_z(exchange_z(sum_y(deal(pieces, "y"))))
    part = exchange_z(copies).reshape(NZ * SUB, RIDE)
    gram = jnp.concatenate([gram, swap(gram)], axis=0)
    gram = collect(collect(gram, "x", NX), "y", NY)
    part, gram = lax.optimization_barrier((part, gram))
    inverse, basis, resident = factor_last(*factor_first(gram), in_hbm(panels), columns)
    reduced, top = update(inverse, basis, every(part, "y", NY), resident)
    return jnp.transpose(reduced, (1, 0, 2)), jnp.transpose(top, (1, 0, 2))


def solution(mesh):
    fine = Mesh(mesh.devices.reshape(NZ, NY, NX, NC), ("z", "y", "x", "c"))
    return jax.shard_map(
        shards,
        mesh=fine,
        in_specs=(P(("z", "y"), None, ("x", "c")),),
        out_specs=(P(("z", "y"), None, ("x", "c")), P(None, None, ("x", "c"))),
        check_vma=False,
    )
```

```python
import jax
import jax.numpy as jnp
from jax import lax
from jax.experimental import pallas as pl
from jax.experimental.pallas import tpu as pltpu
from jax.sharding import Mesh, PartitionSpec as P

PRECISE = lax.Precision.HIGHEST
NZ, NY, NX, NC = 8, 4, 4, 2
LANES, SUB = 128, 8
RIDE = 1280
NT = (((1,), (1,)), ((), ()))
VMEM = pl.BlockSpec(memory_space=pltpu.VMEM)
HBM = pl.BlockSpec(memory_space=pltpu.HBM)


def in_hbm(values):
    return pltpu.with_memory_space_constraint(values, pltpu.HBM)


def params(mib):
    return pltpu.CompilerParams(vmem_limit_bytes=mib << 20)


def dot(left, right, dims=(((1,), (0,)), ((), ()))):
    return lax.dot_general(left, right, dims, precision=PRECISE, preferred_element_type=jnp.float32)


def split(values):
    high = values.astype(jnp.bfloat16)
    return high, (values - high.astype(jnp.float32)).astype(jnp.bfloat16)


def wide_left(values):
    high, low = split(values)
    return jnp.concatenate([high, high, low], axis=1)


def wide_right(values):
    high, low = split(values)
    return jnp.concatenate([high, low, high], axis=0)


def narrow_dot(left, right):
    return lax.dot_general(left, right, (((1,), (0,)), ((), ())), preferred_element_type=jnp.float32)


def pick(index, choices):
    value = choices[-1]
    for at in range(len(choices) - 2, -1, -1):
        value = jnp.where(index == at, choices[at], value)
    return value


def swap(values):
    return lax.ppermute(values, "c", [(0, 1), (1, 0)])


def relay(own):
    x = lax.axis_index("x")
    half = own.shape[0] // 2
    low, high = own[:half], own[half:]
    up_low = lax.ppermute(low, "x", [(0, 1)])
    down_high = lax.ppermute(high, "x", [(0, 3)])
    up_high = lax.ppermute(high, "x", [(0, 1)])
    down_low = lax.ppermute(low, "x", [(0, 3)])
    on_low = lax.ppermute(up_low, "x", [(1, 2)])
    on_high = lax.ppermute(down_high, "x", [(3, 2)])
    mine_low = pick(x, [low, up_low, on_low, down_low])
    mine_high = pick(x, [high, up_high, on_high, down_high])
    return mine_low, mine_high, swap(mine_low), swap(mine_high)


def index_of(axis):
    return lax.axis_index(axis).astype(jnp.int32)[None]


SCALAR = pl.BlockSpec(memory_space=pltpu.SMEM)


def place(core, pieces, p_ref):
    half, k = pieces[0].shape
    first = core == 0
    for at in range(2):
        rows = slice(at * half, (at + 1) * half)
        mine, other = pieces[at][...], pieces[2 + at][...]
        p_ref[rows, :k] = jnp.where(first, mine, other)
        p_ref[rows, k:] = jnp.where(first, other, mine)


def around(at_ref, by, size, rows, base=0):
    return pl.ds(pl.multiple_of(base + ((at_ref[0] + by) % size) * rows, SUB), rows)


def fetch(source, target, sem):
    copies = [pltpu.make_async_copy(source.at[r], target.at[r], sem.at[r]) for r in range(source.shape[0])]
    for copy in copies:
        copy.start()
    return copies


def products_kernel(
    x_ref, y_ref, core_ref, ml_ref, mh_ref, ol_ref, oh_ref, c_hbm, o0_ref, o1_ref, o2_ref, o3_ref, p_hbm, c_ref, p_ref, t_ref, sem, p_sem
):
    rounds, n, k = c_ref.shape
    w = 2 * k
    arriving = fetch(c_hbm, c_ref, sem)
    place(core_ref[0], (ml_ref, mh_ref, ol_ref, oh_ref), p_ref)
    leaving = pltpu.make_async_copy(p_ref, p_hbm, p_sem)
    leaving.start()
    t_ref[...] = p_ref[...].T
    outs = (o0_ref, o1_ref, o2_ref, o3_ref)
    part = w // NY
    left = wide_left(jnp.concatenate([t_ref[around(y_ref, by, NY, part), :] for by in range(NY)], axis=0))
    base = (x_ref[0] * NC + core_ref[0]) * (NY * SUB)
    rows = [t_ref[around(y_ref, by, NY, SUB, base), :] for by in range(NY)]
    gram = dot(jnp.concatenate(rows, axis=0), p_ref[...])
    for by, o_ref in enumerate(outs):
        piece = gram[by * SUB : (by + 1) * SUB]
        o_ref[:, RIDE:] = jnp.zeros((part, LANES), jnp.float32)
        o_ref[:SUB, RIDE:] = piece[:, :LANES]
        o_ref[SUB : 2 * SUB, RIDE:] = piece[:, LANES:]
    group = rounds // 2
    for r in range(0, rounds, group):
        for copy in arriving[r : r + group]:
            copy.wait()
        some = jnp.concatenate([c_ref[at] for at in range(r, r + group)], axis=1)
        cross = narrow_dot(left, wide_right(some))
        for by, o_ref in enumerate(outs):
            o_ref[:, r * k : (r + group) * k] = cross[by * part : (by + 1) * part]
    leaving.wait()


def products(pieces, columns):
    rounds, n, k = columns.shape
    w = 2 * k
    return pl.pallas_call(
        products_kernel,
        in_specs=[SCALAR] * 3 + [VMEM] * 4 + [HBM],
        out_specs=[VMEM] * NY + [HBM],
        out_shape=[jax.ShapeDtypeStruct((w // NY, RIDE + LANES), jnp.float32)] * NY
        + [jax.ShapeDtypeStruct((n, w), jnp.float32)],
        scratch_shapes=[
            pltpu.VMEM(columns.shape, jnp.float32),
            pltpu.VMEM((n, w), jnp.float32),
            pltpu.VMEM((w, n), jnp.float32),
            pltpu.SemaphoreType.DMA((rounds,)),
            pltpu.SemaphoreType.DMA(()),
        ],
        compiler_params=params(20),
        name="products",
    )(index_of("x"), index_of("y"), index_of("c"), *pieces, columns)


def sum_y_kernel(a0_ref, a1_ref, a2_ref, a3_ref, o_ref):
    total = (a0_ref[...] + a1_ref[...]) + (a2_ref[...] + a3_ref[...])
    for z in range(NZ):
        o_ref[z, :, :RIDE] = total[z * SUB : (z + 1) * SUB, :RIDE]
        o_ref[z, :, RIDE : RIDE + LANES] = total[:SUB, RIDE:]
        o_ref[z, :, RIDE + LANES :] = total[SUB : 2 * SUB, RIDE:]


def sum_y(pieces):
    return pl.pallas_call(
        sum_y_kernel,
        in_specs=[VMEM] * NY,
        out_specs=VMEM,
        out_shape=jax.ShapeDtypeStruct((NZ, SUB, RIDE + 2 * LANES), jnp.float32),
        compiler_params=params(4),
        name="sum_y",
    )(*pieces)


def sum_z_kernel(a_ref, o_ref, g_ref):
    total = a_ref[0]
    for z in range(1, NZ):
        total = total + a_ref[z]
    for z in range(NZ):
        o_ref[z] = total[:, :RIDE]
    g_ref[...] = total[:, RIDE:]


def sum_z(pieces):
    return pl.pallas_call(
        sum_z_kernel,
        in_specs=[VMEM],
        out_specs=[VMEM] * 2,
        out_shape=[
            jax.ShapeDtypeStruct((NZ, SUB, RIDE), jnp.float32),
            jax.ShapeDtypeStruct((SUB, 2 * LANES), jnp.float32),
        ],
        compiler_params=params(4),
        name="sum_z",
    )(pieces)


def deal(pieces, axis):
    size = len(pieces)
    return [pieces[0]] + [
        lax.ppermute(pieces[by], axis, [(at, (at + by) % size) for at in range(size)]) for by in range(1, size)
    ]


def every(values, axis, size):
    return [values] + [
        lax.ppermute(values, axis, [(at, (at - by) % size) for at in range(size)]) for by in range(1, size)
    ]


def collect(values, axis, size):
    return jnp.concatenate(every(values, axis, size), axis=0)


def inverse_root(d):
    y = lax.rsqrt(d)
    return y * (1.5 - 0.5 * d * y * y)


def sum4(left, right):
    return (left[0] * right[0] + left[1] * right[1]) + (left[2] * right[2] + left[3] * right[3])


class Pivot:
    def __init__(self, d):
        det = 1.0 / (d[0][0] * d[1][1] - d[1][0] * d[1][0])
        self.p = p00, p01, p11 = d[1][1] * det, -d[1][0] * det, d[0][0] * det
        self.z = z = [[d[r][0] * p00 + d[r][1] * p01, d[r][0] * p01 + d[r][1] * p11] for r in (2, 3)]
        s00 = d[2][2] - (z[0][0] * d[2][0] + z[0][1] * d[2][1])
        s01 = d[3][2] - (z[1][0] * d[2][0] + z[1][1] * d[2][1])
        s11 = d[3][3] - (z[1][0] * d[3][0] + z[1][1] * d[3][1])
        sdet = 1.0 / (s00 * s11 - s01 * s01)
        self.i = s11 * sdet, -s01 * sdet, s00 * sdet
        self.d, self.s = d, (s00, s01, s11)

    def lower(self, r):
        z = self.z
        return [r[2 + at] - (z[at][0] * r[0] + z[at][1] * r[1]) for at in range(2)]

    def solve(self, r):
        (p00, p01, p11), (i00, i01, i11), z = self.p, self.i, self.z
        v2, v3 = self.lower(r)
        y2, y3 = i00 * v2 + i01 * v3, i01 * v2 + i11 * v3
        u0, u1 = p00 * r[0] + p01 * r[1], p01 * r[0] + p11 * r[1]
        return [u0 - (z[0][0] * y2 + z[1][0] * y3), u1 - (z[0][1] * y2 + z[1][1] * y3), y2, y3]

    def rows(self, r):
        d, (s00, s01, s11) = self.d, self.s
        k0 = inverse_root(d[0][0])
        l10 = d[1][0] * k0
        w0 = k0 * r[0]
        w1 = inverse_root(d[1][1] - l10 * l10) * (r[1] - l10 * w0)
        k2 = inverse_root(s00)
        l32 = s01 * k2
        v2, v3 = self.lower(r)
        w2 = k2 * v2
        return [w0, w1, w2, inverse_root(s11 - l32 * l32) * (v3 - l32 * w2)]


def invert_factor(block, w_ref, row0, col0):
    n = LANES
    tiles = n // SUB
    a = [block[SUB * t : SUB * (t + 1)] for t in range(tiles)]
    lane = lax.broadcasted_iota(jnp.int32, (SUB, LANES), 1)
    sub = lax.broadcasted_iota(jnp.int32, (SUB, LANES), 0)
    b = [jnp.where(lane == sub + SUB * t, 1.0, 0.0).astype(jnp.float32) for t in range(tiles)]

    def across(v, j):
        return jnp.broadcast_to(v[:, j : j + 1], (SUB, LANES))

    def down(v, s):
        return jnp.broadcast_to(v[s : s + 1, :], (SUB, LANES))

    for t in range(tiles):
        j = SUB * t
        columns = [across(a[t], j + k) for k in range(SUB)]
        d = [[down(columns[y], x) for y in range(SUB)] for x in range(SUB)]
        ra = [down(a[t], k) for k in range(SUB)]
        rb = [down(b[t], k) for k in range(SUB)]
        head = Pivot([row[:4] for row in d[:4]])
        g = [head.solve([d[y][k] for k in range(4)]) for y in range(4, SUB)]
        rest = [[None] * 4 for _ in range(4)]
        for x in range(4):
            for y in range(x + 1):
                rest[x][y] = rest[y][x] = d[4 + x][4 + y] - sum4(d[4 + x][:4], g[y])
        tail = Pivot(rest)
        za, zb, low_b = [], [], None
        for r, z in ((ra, za), (rb, zb)):
            low = [r[4 + x] - sum4(g[x], r[:4]) for x in range(4)]
            y1, y2 = head.solve(r[:4]), tail.solve(low)
            z += [y1[k] - sum4([g[x][k] for x in range(4)], y2) for k in range(4)] + y2
            low_b = low
        for u in range(t + 1, tiles):
            c = [across(a[u], j + k) for k in range(SUB)]
            a[u], b[u] = (
                v - (sum4(c[:4], z[:4]) + sum4(c[4:], z[4:])) for v, z in ((a[u], za), (b[u], zb))
            )
        for k, w in enumerate(head.rows(rb[:4]) + tail.rows(low_b)):
            w_ref[row0 + j + k : row0 + j + k + 1, col0 : col0 + LANES] = w[0:1]


def factor_first_kernel(x_ref, y_ref, core_ref, p_ref, w_ref, l_ref, s_ref, g_ref):
    h = LANES
    for dy in range(NY):
        for dc in range(NC):
            for dx in range(NX):
                x, y, core = (x_ref[0] + dx) % NX, (y_ref[0] + dy) % NY, (core_ref[0] + dc) % NC
                at = pl.multiple_of(((x * NC + core) * NY + y) * SUB, SUB)
                row = ((dy * NC + dc) * NX + dx) * SUB
                g_ref[pl.ds(at, SUB), :] = p_ref[row : row + SUB, :]
    invert_factor(g_ref[:h, :h], w_ref, 0, 0)
    l21 = dot(g_ref[h:, :h], w_ref[...], NT)
    l_ref[...] = l21
    s_ref[...] = g_ref[h:, h:] - dot(l21, l21, NT)


def factor_last_kernel(w11_ref, l_ref, s_ref, p_hbm, c_hbm, w_ref, q_ref, c_ref, p_ref, sem, c_sem):
    arriving = pltpu.make_async_copy(p_hbm, p_ref, sem)
    arriving.start()
    resident = pltpu.make_async_copy(c_hbm, c_ref, c_sem)
    resident.start()
    h = LANES
    w11 = w11_ref[...]
    w_ref[:h, :h] = w11
    w_ref[:h, h:] = jnp.zeros((h, h), jnp.float32)
    invert_factor(s_ref[...], w_ref, h, h)
    w_ref[h:, :h] = -dot(w_ref[h:, h:], dot(l_ref[...], w11))
    arriving.wait()
    high, low = split(w_ref[...])
    right = jnp.concatenate([high, low, high], axis=1)
    basis = lax.dot_general(wide_left(p_ref[...]), right, NT, preferred_element_type=jnp.float32)
    q_ref[...] = wide_left(basis)
    resident.wait()


def factor_first(pieces):
    w = pieces.shape[0]
    h = w // 2
    return pl.pallas_call(
        factor_first_kernel,
        in_specs=[SCALAR] * 3 + [VMEM],
        out_specs=[VMEM] * 3,
        out_shape=[jax.ShapeDtypeStruct((h, h), jnp.float32)] * 3,
        scratch_shapes=[pltpu.VMEM((w, w), jnp.float32)],
        compiler_params=params(8),
        name="factor_first",
    )(index_of("x"), index_of("y"), index_of("c"), pieces)


def factor_last(w11, l21, schur, panels, columns):
    n, w = panels.shape
    return pl.pallas_call(
        factor_last_kernel,
        in_specs=[VMEM] * 3 + [HBM] * 2,
        out_specs=[VMEM] * 3,
        out_shape=[
            jax.ShapeDtypeStruct((w, w), jnp.float32),
            jax.ShapeDtypeStruct((n, 3 * w), jnp.bfloat16),
            jax.ShapeDtypeStruct(columns.shape, jnp.float32),
        ],
        scratch_shapes=[
            pltpu.VMEM((n, w), jnp.float32),
            pltpu.SemaphoreType.DMA(()),
            pltpu.SemaphoreType.DMA(()),
        ],
        compiler_params=params(12),
        name="factor_last",
    )(w11, l21, schur, panels, columns)


BAND = 256


def update_kernel(
    y_ref, w_ref, q_ref, x0_ref, x1_ref, x2_ref, x3_ref, c_ref, red_hbm, top_hbm, x_ref, red_ref, top_ref, red_sem, top_sem
):
    rounds, n, k = red_ref.shape
    bands = [pl.ds(at, BAND) for at in range(0, n, BAND)]
    for by, part_ref in enumerate((x0_ref, x1_ref, x2_ref, x3_ref)):
        x_ref[around(y_ref, by, NY, part_ref.shape[0]), :] = part_ref[...]
    top = narrow_dot(wide_left(w_ref[...]), wide_right(x_ref[...]))
    for r in range(rounds):
        top_ref[r] = top[:, r * k : (r + 1) * k]
    leaving = [pltpu.make_async_copy(top_ref, top_hbm, top_sem)]
    leaving[0].start()
    right = wide_right(top)
    for at, band in enumerate(bands):
        fit = narrow_dot(q_ref[at * BAND : (at + 1) * BAND], right)
        rows = slice(at * BAND, (at + 1) * BAND)
        for r in range(rounds):
            red_ref[r, rows] = c_ref[r, rows] - fit[:, r * k : (r + 1) * k]
        copy = pltpu.make_async_copy(red_ref.at[:, band], red_hbm.at[:, band], red_sem.at[at])
        copy.start()
        leaving.append(copy)
    for copy in leaving:
        copy.wait()


def update(inverse, basis, cross, columns):
    rounds, n, k = columns.shape
    w = inverse.shape[0]
    reduced, top = (rounds, n, k), (rounds, w, k)
    return pl.pallas_call(
        update_kernel,
        in_specs=[SCALAR] + [VMEM] * (3 + NY),
        out_specs=[HBM] * 2,
        out_shape=[jax.ShapeDtypeStruct(reduced, jnp.float32), jax.ShapeDtypeStruct(top, jnp.float32)],
        scratch_shapes=[
            pltpu.VMEM((w, rounds * k), jnp.float32),
            pltpu.VMEM(reduced, jnp.float32),
            pltpu.VMEM(top, jnp.float32),
            pltpu.SemaphoreType.DMA((n // BAND,)),
            pltpu.SemaphoreType.DMA(()),
        ],
        compiler_params=params(24),
        name="update",
    )(index_of("y"), inverse, basis, *cross, columns)


def exchange_z(pieces):
    return lax.all_to_all(pieces, "z", 0, 0)


def shards(matrix):
    columns = jnp.transpose(matrix, (1, 0, 2))
    own, columns = columns[0], in_hbm(columns)
    *pieces, panels = products(relay(own), columns)
    copies, gram = sum_z(exchange_z(sum_y(deal(pieces, "y"))))
    part = exchange_z(copies).reshape(NZ * SUB, RIDE)
    gram = collect(gram, "x", NX)
    gram = collect(jnp.concatenate([gram, swap(gram)], axis=0), "y", NY)
    part, gram = lax.optimization_barrier((part, gram))
    inverse, basis, resident = factor_last(*factor_first(gram), in_hbm(panels), columns)
    reduced, top = update(inverse, basis, every(part, "y", NY), resident)
    return jnp.transpose(reduced, (1, 0, 2)), jnp.transpose(top, (1, 0, 2))


def solution(mesh):
    fine = Mesh(mesh.devices.reshape(NZ, NY, NX, NC), ("z", "y", "x", "c"))
    return jax.shard_map(
        shards,
        mesh=fine,
        in_specs=(P(("z", "y"), None, ("x", "c")),),
        out_specs=(P(("z", "y"), None, ("x", "c")), P(None, None, ("x", "c"))),
        check_vma=False,
    )
```

```python
import jax
import jax.numpy as jnp
from jax import lax
from jax.experimental import pallas as pl
from jax.experimental.pallas import tpu as pltpu
from jax.sharding import Mesh, PartitionSpec as P

PRECISE = lax.Precision.HIGHEST
NZ, NY, NX, NC = 8, 4, 4, 2
LANES, SUB = 128, 8
RIDE = 1280
NT = (((1,), (1,)), ((), ()))
VMEM = pl.BlockSpec(memory_space=pltpu.VMEM)
HBM = pl.BlockSpec(memory_space=pltpu.HBM)


def in_hbm(values):
    return pltpu.with_memory_space_constraint(values, pltpu.HBM)


def params(mib):
    return pltpu.CompilerParams(vmem_limit_bytes=mib << 20)


def dot(left, right, dims=(((1,), (0,)), ((), ()))):
    return lax.dot_general(left, right, dims, precision=PRECISE, preferred_element_type=jnp.float32)


def split(values):
    high = values.astype(jnp.bfloat16)
    return high, (values - high.astype(jnp.float32)).astype(jnp.bfloat16)


def wide_left(values):
    high, low = split(values)
    return jnp.concatenate([high, high, low], axis=1)


def wide_right(values):
    high, low = split(values)
    return jnp.concatenate([high, low, high], axis=0)


def narrow_dot(left, right):
    return lax.dot_general(left, right, (((1,), (0,)), ((), ())), preferred_element_type=jnp.float32)


def pick(index, choices):
    value = choices[-1]
    for at in range(len(choices) - 2, -1, -1):
        value = jnp.where(index == at, choices[at], value)
    return value


def swap(values):
    return lax.ppermute(values, "c", [(0, 1), (1, 0)])


def relay(own):
    x = lax.axis_index("x")
    half = own.shape[0] // 2
    low, high = own[:half], own[half:]
    up_low = lax.ppermute(low, "x", [(0, 1)])
    down_high = lax.ppermute(high, "x", [(0, 3)])
    up_high = lax.ppermute(high, "x", [(0, 1)])
    down_low = lax.ppermute(low, "x", [(0, 3)])
    on_low = lax.ppermute(up_low, "x", [(1, 2)])
    on_high = lax.ppermute(down_high, "x", [(3, 2)])
    mine_low = pick(x, [low, up_low, on_low, down_low])
    mine_high = pick(x, [high, up_high, on_high, down_high])
    return mine_low, mine_high, swap(mine_low), swap(mine_high)


def index_of(axis):
    return lax.axis_index(axis).astype(jnp.int32)[None]


SCALAR = pl.BlockSpec(memory_space=pltpu.SMEM)


def place(core, pieces, p_ref):
    half, k = pieces[0].shape
    first = core == 0
    for at in range(2):
        rows = slice(at * half, (at + 1) * half)
        mine, other = pieces[at][...], pieces[2 + at][...]
        p_ref[rows, :k] = jnp.where(first, mine, other)
        p_ref[rows, k:] = jnp.where(first, other, mine)


def around(at_ref, by, size, rows, base=0):
    return pl.ds(pl.multiple_of(base + ((at_ref[0] + by) % size) * rows, SUB), rows)


def fetch(source, target, sem):
    copies = [pltpu.make_async_copy(source.at[r], target.at[r], sem.at[r]) for r in range(source.shape[0])]
    for copy in copies:
        copy.start()
    return copies


def products_kernel(
    x_ref, y_ref, core_ref, ml_ref, mh_ref, ol_ref, oh_ref, c_hbm, o0_ref, o1_ref, o2_ref, o3_ref, p_hbm, c_ref, p_ref, t_ref, sem, p_sem
):
    rounds, n, k = c_ref.shape
    w = 2 * k
    arriving = fetch(c_hbm, c_ref, sem)
    place(core_ref[0], (ml_ref, mh_ref, ol_ref, oh_ref), p_ref)
    leaving = pltpu.make_async_copy(p_ref, p_hbm, p_sem)
    leaving.start()
    t_ref[...] = p_ref[...].T
    outs = (o0_ref, o1_ref, o2_ref, o3_ref)
    part = w // NY
    left = wide_left(jnp.concatenate([t_ref[around(y_ref, by, NY, part), :] for by in range(NY)], axis=0))
    base = (x_ref[0] * NC + core_ref[0]) * (NY * SUB)
    rows = [t_ref[around(y_ref, by, NY, SUB, base), :] for by in range(NY)]
    gram = dot(jnp.concatenate(rows, axis=0), p_ref[...])
    for by, o_ref in enumerate(outs):
        piece = gram[by * SUB : (by + 1) * SUB]
        o_ref[:, RIDE:] = jnp.zeros((part, LANES), jnp.float32)
        o_ref[:SUB, RIDE:] = piece[:, :LANES]
        o_ref[SUB : 2 * SUB, RIDE:] = piece[:, LANES:]
    group = rounds // 2
    for r in range(0, rounds, group):
        for copy in arriving[r : r + group]:
            copy.wait()
        some = jnp.concatenate([c_ref[at] for at in range(r, r + group)], axis=1)
        cross = narrow_dot(left, wide_right(some))
        for by, o_ref in enumerate(outs):
            o_ref[:, r * k : (r + group) * k] = cross[by * part : (by + 1) * part]
    leaving.wait()


def products(pieces, columns):
    rounds, n, k = columns.shape
    w = 2 * k
    return pl.pallas_call(
        products_kernel,
        in_specs=[SCALAR] * 3 + [VMEM] * 4 + [HBM],
        out_specs=[VMEM] * NY + [HBM],
        out_shape=[jax.ShapeDtypeStruct((w // NY, RIDE + LANES), jnp.float32)] * NY
        + [jax.ShapeDtypeStruct((n, w), jnp.float32)],
        scratch_shapes=[
            pltpu.VMEM(columns.shape, jnp.float32),
            pltpu.VMEM((n, w), jnp.float32),
            pltpu.VMEM((w, n), jnp.float32),
            pltpu.SemaphoreType.DMA((rounds,)),
            pltpu.SemaphoreType.DMA(()),
        ],
        compiler_params=params(20),
        name="products",
    )(index_of("x"), index_of("y"), index_of("c"), *pieces, columns)


def sum_y_kernel(a0_ref, a1_ref, a2_ref, a3_ref, o_ref):
    total = (a0_ref[...] + a1_ref[...]) + (a2_ref[...] + a3_ref[...])
    for z in range(NZ):
        o_ref[z, :, :RIDE] = total[z * SUB : (z + 1) * SUB, :RIDE]
        o_ref[z, :, RIDE : RIDE + LANES] = total[:SUB, RIDE:]
        o_ref[z, :, RIDE + LANES :] = total[SUB : 2 * SUB, RIDE:]


def sum_y(pieces):
    return pl.pallas_call(
        sum_y_kernel,
        in_specs=[VMEM] * NY,
        out_specs=VMEM,
        out_shape=jax.ShapeDtypeStruct((NZ, SUB, RIDE + 2 * LANES), jnp.float32),
        compiler_params=params(4),
        name="sum_y",
    )(*pieces)


def sum_z_kernel(a_ref, o_ref, g_ref):
    total = a_ref[0]
    for z in range(1, NZ):
        total = total + a_ref[z]
    for z in range(NZ):
        o_ref[z] = total[:, :RIDE]
    g_ref[...] = total[:, RIDE:]


def sum_z(pieces):
    return pl.pallas_call(
        sum_z_kernel,
        in_specs=[VMEM],
        out_specs=[VMEM] * 2,
        out_shape=[
            jax.ShapeDtypeStruct((NZ, SUB, RIDE), jnp.float32),
            jax.ShapeDtypeStruct((SUB, 2 * LANES), jnp.float32),
        ],
        compiler_params=params(4),
        name="sum_z",
    )(pieces)


def deal(pieces, axis):
    size = len(pieces)
    return [pieces[0]] + [
        lax.ppermute(pieces[by], axis, [(at, (at + by) % size) for at in range(size)]) for by in range(1, size)
    ]


def every(values, axis, size):
    return [values] + [
        lax.ppermute(values, axis, [(at, (at - by) % size) for at in range(size)]) for by in range(1, size)
    ]


def collect(values, axis, size):
    return jnp.concatenate(every(values, axis, size), axis=0)


def inverse_root(d):
    y = lax.rsqrt(d)
    return y * (1.5 - 0.5 * d * y * y)


def sum4(left, right):
    return (left[0] * right[0] + left[1] * right[1]) + (left[2] * right[2] + left[3] * right[3])


class Pivot:
    def __init__(self, d):
        det = 1.0 / (d[0][0] * d[1][1] - d[1][0] * d[1][0])
        self.p = p00, p01, p11 = d[1][1] * det, -d[1][0] * det, d[0][0] * det
        self.z = z = [[d[r][0] * p00 + d[r][1] * p01, d[r][0] * p01 + d[r][1] * p11] for r in (2, 3)]
        s00 = d[2][2] - (z[0][0] * d[2][0] + z[0][1] * d[2][1])
        s01 = d[3][2] - (z[1][0] * d[2][0] + z[1][1] * d[2][1])
        s11 = d[3][3] - (z[1][0] * d[3][0] + z[1][1] * d[3][1])
        sdet = 1.0 / (s00 * s11 - s01 * s01)
        self.i = s11 * sdet, -s01 * sdet, s00 * sdet
        self.d, self.s = d, (s00, s01, s11)

    def lower(self, r):
        z = self.z
        return [r[2 + at] - (z[at][0] * r[0] + z[at][1] * r[1]) for at in range(2)]

    def solve(self, r):
        (p00, p01, p11), (i00, i01, i11), z = self.p, self.i, self.z
        v2, v3 = self.lower(r)
        y2, y3 = i00 * v2 + i01 * v3, i01 * v2 + i11 * v3
        u0, u1 = p00 * r[0] + p01 * r[1], p01 * r[0] + p11 * r[1]
        return [u0 - (z[0][0] * y2 + z[1][0] * y3), u1 - (z[0][1] * y2 + z[1][1] * y3), y2, y3]

    def rows(self, r):
        d, (s00, s01, s11) = self.d, self.s
        k0 = inverse_root(d[0][0])
        l10 = d[1][0] * k0
        w0 = k0 * r[0]
        w1 = inverse_root(d[1][1] - l10 * l10) * (r[1] - l10 * w0)
        k2 = inverse_root(s00)
        l32 = s01 * k2
        v2, v3 = self.lower(r)
        w2 = k2 * v2
        return [w0, w1, w2, inverse_root(s11 - l32 * l32) * (v3 - l32 * w2)]


def invert_factor(block, w_ref, row0, col0):
    n = LANES
    tiles = n // SUB
    a = [block[SUB * t : SUB * (t + 1)] for t in range(tiles)]
    lane = lax.broadcasted_iota(jnp.int32, (SUB, LANES), 1)
    sub = lax.broadcasted_iota(jnp.int32, (SUB, LANES), 0)
    b = [jnp.where(lane == sub + SUB * t, 1.0, 0.0).astype(jnp.float32) for t in range(tiles)]

    def across(v, j):
        return jnp.broadcast_to(v[:, j : j + 1], (SUB, LANES))

    def down(v, s):
        return jnp.broadcast_to(v[s : s + 1, :], (SUB, LANES))

    for t in range(tiles):
        j = SUB * t
        columns = [across(a[t], j + k) for k in range(SUB)]
        d = [[down(columns[y], x) for y in range(SUB)] for x in range(SUB)]
        ra = [down(a[t], k) for k in range(SUB)]
        rb = [down(b[t], k) for k in range(SUB)]
        head = Pivot([row[:4] for row in d[:4]])
        g = [head.solve([d[y][k] for k in range(4)]) for y in range(4, SUB)]
        rest = [[None] * 4 for _ in range(4)]
        for x in range(4):
            for y in range(x + 1):
                rest[x][y] = rest[y][x] = d[4 + x][4 + y] - sum4(d[4 + x][:4], g[y])
        tail = Pivot(rest)
        za, zb, low_b = [], [], None
        for r, z in ((ra, za), (rb, zb)):
            low = [r[4 + x] - sum4(g[x], r[:4]) for x in range(4)]
            y1, y2 = head.solve(r[:4]), tail.solve(low)
            z += [y1[k] - sum4([g[x][k] for x in range(4)], y2) for k in range(4)] + y2
            low_b = low
        for u in range(t + 1, tiles):
            c = [across(a[u], j + k) for k in range(SUB)]
            a[u], b[u] = (
                v - (sum4(c[:4], z[:4]) + sum4(c[4:], z[4:])) for v, z in ((a[u], za), (b[u], zb))
            )
        for k, w in enumerate(head.rows(rb[:4]) + tail.rows(low_b)):
            w_ref[row0 + j + k : row0 + j + k + 1, col0 : col0 + LANES] = w[0:1]


def factor_kernel(x_ref, y_ref, core_ref, pieces_ref, p_hbm, c_hbm, w_ref, q_ref, c_ref, g_ref, p_ref, sem, c_sem):
    arriving = pltpu.make_async_copy(p_hbm, p_ref, sem)
    arriving.start()
    resident = pltpu.make_async_copy(c_hbm, c_ref, c_sem)
    resident.start()
    h = LANES
    for dy in range(NY):
        for dc in range(NC):
            for dx in range(NX):
                x, y, core = (x_ref[0] + dx) % NX, (y_ref[0] + dy) % NY, (core_ref[0] + dc) % NC
                at = pl.multiple_of(((x * NC + core) * NY + y) * SUB, SUB)
                row = ((dy * NC + dc) * NX + dx) * SUB
                g_ref[pl.ds(at, SUB), :] = pieces_ref[row : row + SUB, :]
    invert_factor(g_ref[:h, :h], w_ref, 0, 0)
    w_ref[:h, h:] = jnp.zeros((h, h), jnp.float32)
    w11 = w_ref[:h, :h]
    l21 = dot(g_ref[h:, :h], w11, NT)
    invert_factor(g_ref[h:, h:] - dot(l21, l21, NT), w_ref, h, h)
    w_ref[h:, :h] = -dot(w_ref[h:, h:], dot(l21, w11))
    high, low = split(w_ref[...])
    right = jnp.concatenate([high, low, high], axis=1)
    arriving.wait()
    basis = lax.dot_general(wide_left(p_ref[...]), right, NT, preferred_element_type=jnp.float32)
    q_ref[...] = wide_left(basis)
    resident.wait()


def factor(pieces, panels, columns):
    n, w = panels.shape
    return pl.pallas_call(
        factor_kernel,
        in_specs=[SCALAR] * 3 + [VMEM] + [HBM] * 2,
        out_specs=[VMEM] * 3,
        out_shape=[
            jax.ShapeDtypeStruct((w, w), jnp.float32),
            jax.ShapeDtypeStruct((n, 3 * w), jnp.bfloat16),
            jax.ShapeDtypeStruct(columns.shape, jnp.float32),
        ],
        scratch_shapes=[
            pltpu.VMEM((w, w), jnp.float32),
            pltpu.VMEM((n, w), jnp.float32),
            pltpu.SemaphoreType.DMA(()),
            pltpu.SemaphoreType.DMA(()),
        ],
        compiler_params=params(12),
        name="factor",
    )(index_of("x"), index_of("y"), index_of("c"), pieces, panels, columns)


BAND = 256


def update_kernel(
    y_ref, w_ref, q_ref, x0_ref, x1_ref, x2_ref, x3_ref, c_ref, red_hbm, top_hbm, x_ref, red_ref, top_ref, red_sem, top_sem
):
    rounds, n, k = red_ref.shape
    bands = [pl.ds(at, BAND) for at in range(0, n, BAND)]
    for by, part_ref in enumerate((x0_ref, x1_ref, x2_ref, x3_ref)):
        x_ref[around(y_ref, by, NY, part_ref.shape[0]), :] = part_ref[...]
    top = narrow_dot(wide_left(w_ref[...]), wide_right(x_ref[...]))
    for r in range(rounds):
        top_ref[r] = top[:, r * k : (r + 1) * k]
    leaving = [pltpu.make_async_copy(top_ref, top_hbm, top_sem)]
    leaving[0].start()
    right = wide_right(top)
    for at, band in enumerate(bands):
        fit = narrow_dot(q_ref[at * BAND : (at + 1) * BAND], right)
        rows = slice(at * BAND, (at + 1) * BAND)
        for r in range(rounds):
            red_ref[r, rows] = c_ref[r, rows] - fit[:, r * k : (r + 1) * k]
        copy = pltpu.make_async_copy(red_ref.at[:, band], red_hbm.at[:, band], red_sem.at[at])
        copy.start()
        leaving.append(copy)
    for copy in leaving:
        copy.wait()


def update(inverse, basis, cross, columns):
    rounds, n, k = columns.shape
    w = inverse.shape[0]
    reduced, top = (rounds, n, k), (rounds, w, k)
    return pl.pallas_call(
        update_kernel,
        in_specs=[SCALAR] + [VMEM] * (3 + NY),
        out_specs=[HBM] * 2,
        out_shape=[jax.ShapeDtypeStruct(reduced, jnp.float32), jax.ShapeDtypeStruct(top, jnp.float32)],
        scratch_shapes=[
            pltpu.VMEM((w, rounds * k), jnp.float32),
            pltpu.VMEM(reduced, jnp.float32),
            pltpu.VMEM(top, jnp.float32),
            pltpu.SemaphoreType.DMA((n // BAND,)),
            pltpu.SemaphoreType.DMA(()),
        ],
        compiler_params=params(24),
        name="update",
    )(index_of("y"), inverse, basis, *cross, columns)


def exchange_z(pieces):
    return lax.all_to_all(pieces, "z", 0, 0)


def shards(matrix):
    columns = jnp.transpose(matrix, (1, 0, 2))
    own, columns = columns[0], in_hbm(columns)
    *pieces, panels = products(relay(own), columns)
    copies, gram = sum_z(exchange_z(sum_y(deal(pieces, "y"))))
    part = exchange_z(copies).reshape(NZ * SUB, RIDE)
    gram = collect(gram, "x", NX)
    gram = collect(jnp.concatenate([gram, swap(gram)], axis=0), "y", NY)
    part, gram = lax.optimization_barrier((part, gram))
    inverse, basis, resident = factor(gram, in_hbm(panels), columns)
    reduced, top = update(inverse, basis, every(part, "y", NY), resident)
    return jnp.transpose(reduced, (1, 0, 2)), jnp.transpose(top, (1, 0, 2))


def solution(mesh):
    fine = Mesh(mesh.devices.reshape(NZ, NY, NX, NC), ("z", "y", "x", "c"))
    return jax.shard_map(
        shards,
        mesh=fine,
        in_specs=(P(("z", "y"), None, ("x", "c")),),
        out_specs=(P(("z", "y"), None, ("x", "c")), P(None, None, ("x", "c"))),
        check_vma=False,
    )
```
